256 devices in a mesh: seq: 32 (over z, x), head: 8 (over y, core).
Axes of the slice: x: 4, y: 4, z: 8, core: 2. Of those that a mesh axis runs over, the one named last changes fastest.
Arguments:
- queries: bfloat16 [32768, 4096], P('seq', 'head'), may hold values from -6 to 6
- key_vectors: bfloat16 [32768, 4096], P('seq', 'head'), may hold values from -6 to 6
- value_vectors: bfloat16 [32768, 4096], P('seq', 'head'), may hold values from -6 to 6
- gate_input: bfloat16 [32768, 4096], P('seq', 'head'), may hold values from -6 to 6
- log_decay: float32 [32768, 32], P('seq', 'head'), may hold values from -1.5 to 0, as said below
- out_weight: bfloat16 [4096, 4096], P('head'), may hold values from -0.09375 to 0.09375
Outputs:
- projected: bfloat16 [32768, 4096], P(('seq', 'head'))
The draws below stay inside these ranges and needn't reach their ends.
Inputs may be any that keep to these rules, and one draw needn't show every extreme that they name: `log_decay`: every entry is negative.
All inputs are finite; a program needn't handle non-finite values.
Results may differ from the reference program's by a relative error of at most 0.0054.
Values sent between devices are 32-bit elements; how exact they have to be, the bound alone decides.
A program may use at most 128 MiB of HBM per device.

```python
import math
import jax
import jax.numpy as jnp
from jax import lax

D = 4096
HEAD_COUNT = 32
HEAD_DIM = 128
BLOCK_LEN = 256
TOK_DEV = 1024
SEQUENCE_LENGTH = 32768


def draw_log_decay(key, part):
    every_key = jax.random.split(key, 6)
    fast_share = 0.5
    fast = jax.random.uniform(every_key[0], (HEAD_COUNT,)) < fast_share
    fast_rate = jax.random.uniform(every_key[1], (HEAD_COUNT,), jnp.float32, 1.0 / 50.0, 1.0 / 30.0)
    slow_rate = 0.5 / SEQUENCE_LENGTH
    base = jnp.where(fast, fast_rate, slow_rate)
    block_scale = jnp.exp(jax.random.uniform(every_key[2], (SEQUENCE_LENGTH // TOK_DEV, 1, HEAD_COUNT), jnp.float32, math.log(0.6), math.log(1.4)))
    block_scale = jnp.broadcast_to(block_scale, (SEQUENCE_LENGTH // TOK_DEV, TOK_DEV, HEAD_COUNT)).reshape(SEQUENCE_LENGTH, HEAD_COUNT)
    rough = jax.random.uniform(every_key[3], (SEQUENCE_LENGTH, HEAD_COUNT), jnp.float32, 0.5, 1.5)
    decay_speed = base[None, :] * block_scale * rough
    spike_locations = jax.random.randint(every_key[4], (2, HEAD_COUNT), 0, SEQUENCE_LENGTH)
    spike_penalty = jax.random.uniform(every_key[5], (2, HEAD_COUNT), jnp.float32, 0.2, 0.5)
    token_places = jnp.arange(SEQUENCE_LENGTH, dtype=jnp.int32)[:, None]
    spike_flag = jnp.zeros((SEQUENCE_LENGTH, HEAD_COUNT), jnp.float32)
    for selector_index in range(2):
        spike_flag = spike_flag + jnp.where(token_places == spike_locations[selector_index][None, :], jnp.log(1.0 - spike_penalty[selector_index])[None, :], 0.0)
    return (spike_flag - decay_speed).astype(jnp.float32)


def levels(rng, dims, pieces, smallest, high):
    gain, own = 1.0, jax.random.fold_in(rng, 6)
    for position, shards_of in pieces:
        heights = jnp.exp(jax.random.uniform(jax.random.fold_in(own, position), (shards_of,), jnp.float32, smallest / len(pieces), high / len(pieces)))
        gain = gain * jnp.repeat(heights, dims[position] // shards_of).reshape([-1 if axis == position else 1 for axis in range(len(dims))])
    return gain


def scatter_about(rng, extent, width, most, cuts=(), kind=jnp.bfloat16):
    factor_of = levels(rng, extent, cuts, -0.22, 0.18) if cuts else 1.0
    array = jax.random.normal(rng, extent, jnp.float32) * width * factor_of
    return jnp.minimum(jnp.maximum(array, -most), most).astype(kind)


def setup_inputs(seed: int = 0) -> dict:
    key_of = jax.random.split(jax.random.key(seed), 7)
    return {
        "queries": scatter_about(key_of[0], (SEQUENCE_LENGTH, HEAD_COUNT * HEAD_DIM), 1.0, 6.0, ((0, 32), (1, 8))),
        "key_vectors": scatter_about(key_of[1], (SEQUENCE_LENGTH, HEAD_COUNT * HEAD_DIM), 1.0, 6.0, ((0, 32), (1, 8))),
        "value_vectors": scatter_about(key_of[2], (SEQUENCE_LENGTH, HEAD_COUNT * HEAD_DIM), 1.0, 6.0, ((0, 32), (1, 8))),
        "gate_input": scatter_about(key_of[3], (SEQUENCE_LENGTH, HEAD_COUNT * HEAD_DIM), 1.0, 6.0, ((0, 32), (1, 8))),
        "log_decay": draw_log_decay(jax.random.fold_in(key_of[6], 71), 0),
        "out_weight": scatter_about(key_of[5], (HEAD_COUNT * HEAD_DIM, D), (HEAD_COUNT * HEAD_DIM) ** -0.5, 0.09375, ((0, 8),)),
    }


def reference(queries, key_vectors, value_vectors, gate_input, log_decay, out_weight):
    block_count = SEQUENCE_LENGTH // BLOCK_LEN
    split_shape = (block_count, BLOCK_LEN, HEAD_COUNT, HEAD_DIM)
    token_places = lax.iota(jnp.int32, BLOCK_LEN)
    causal = token_places[:, None] >= token_places[None, :]
    highest = lax.Precision.HIGHEST

    def advance(kv_state, blocks):
        query_block, key_block, value_block, rate_block = blocks
        running = jnp.cumsum(rate_block, axis=0)
        block_total = running[-1]
        query_float = query_block.astype(jnp.float32)
        key_float = key_block.astype(jnp.float32)
        value_float = value_block.astype(jnp.float32)
        scores = jnp.einsum('ihd,jhd->hij', query_float, key_float, precision=highest)
        by_head = running.T
        spread = by_head[:, :, None] - by_head[:, None, :]
        decay = jnp.exp(jnp.where(causal, spread, -1e+30))
        weights = lax.optimization_barrier((scores * decay).astype(jnp.bfloat16)).astype(jnp.float32)
        inside = jnp.einsum('hij,jhd->ihd', weights, value_float, precision=highest)
        query_scaled = query_float * jnp.exp(running)[:, :, None]
        carried = jnp.einsum('ihd,hde->ihe', query_scaled, kv_state, precision=highest)
        key_scaled = key_float * jnp.exp(block_total[None, :] - running)[:, :, None]
        kv_next = jnp.exp(block_total)[:, None, None] * kv_state + jnp.einsum('jhd,jhe->hde', key_scaled, value_float, precision=highest)
        return (kv_next, inside + carried)
    initial = jnp.zeros((HEAD_COUNT, HEAD_DIM, HEAD_DIM), jnp.float32)
    _, attended = lax.scan(advance, initial, (queries.reshape(split_shape), key_vectors.reshape(split_shape), value_vectors.reshape(split_shape), log_decay.reshape(block_count, BLOCK_LEN, HEAD_COUNT)))
    attended = attended.reshape(SEQUENCE_LENGTH, HEAD_COUNT, HEAD_DIM)
    inverse_rms = lax.rsqrt(lax.optimization_barrier(jnp.mean(attended * attended, axis=-1, keepdims=True)) + 1e-06)
    normed = (attended * inverse_rms).reshape(SEQUENCE_LENGTH, HEAD_COUNT * HEAD_DIM)
    hidden = (normed * jax.nn.silu(gate_input.astype(jnp.float32))).astype(jnp.bfloat16)
    hidden_float = lax.optimization_barrier(hidden).astype(jnp.float32)
    projected = jnp.dot(hidden_float, out_weight.astype(jnp.float32), precision=highest)
    return projected.astype(jnp.bfloat16)
```

```python
import functools

import jax
import jax.numpy as jnp
from jax import lax
from jax.experimental import pallas as pl
from jax.experimental.pallas import tpu as pltpu
from jax.sharding import PartitionSpec as P

HEAD_DIM = 128
BLOCK = 256
HALF = 128
HEADS = 4
BLOCKS = 4
FEATURES = HEADS * HEAD_DIM
WIDTH = 4096
CHUNK = 512
CHUNKS = WIDTH // CHUNK
SIDE = CHUNKS // 2
WIDE = 1024
PARTS = WIDTH // WIDE
F32 = jnp.float32
BF16 = jnp.bfloat16
MESH = pl.DeviceIdType.MESH
NT = (((1,), (1,)), ((), ()))
TN = (((0,), (0,)), ((), ()))


def head_columns(h):
    return slice(h * HEAD_DIM, (h + 1) * HEAD_DIM)


def kernel(
    seq_size, rate_hbm, k_hbm, v_hbm, q_hbm, g_hbm, w_hbm, out_ref,
    rate, k, v, q, g, w, w_send, w_recv, w_pair,
    run_col, run_row, start, lead, state_send, state_recv, scan_send, scan_recv,
    att, hid, hid_recv, far, plus, minus, own, far_recv, direct_recv, sum_recv,
    load_sem, a_send, a_recv, b_send, b_recv, w_ssem, w_rsem, h_ssem, h_rsem,
    y_send, y_recv,
):
    me = lax.axis_index("seq")
    head = lax.axis_index("head")
    row = head // 2
    core = lax.rem(head, 2)
    partner = row * 2 + (1 - core)
    up = lax.rem(row + 1, 4) * 2 + core
    down = lax.rem(row + 3, 4) * 2 + core
    slice_rows = FEATURES // seq_size
    per_head = HEAD_DIM // slice_rows

    loads = [
        pltpu.make_async_copy(src, dst, load_sem.at[i])
        for i, (src, dst) in enumerate(
            ((rate_hbm, rate), (k_hbm, k), (v_hbm, v), (q_hbm, q), (w_hbm, w), (g_hbm, g))
        )
    ]
    for load in loads:
        load.start()

    barrier = pltpu.get_barrier_semaphore()

    def greet(d, carry):
        peer = lax.rem(me + d, seq_size)
        pl.semaphore_signal(barrier, inc=1, device_id=(peer, head), device_id_type=MESH)
        return carry

    lax.fori_loop(1, seq_size, greet, 0)
    for other in (partner, up, down):
        pl.semaphore_signal(barrier, inc=1, device_id=(me, other), device_id_type=MESH)

    low = lax.broadcasted_iota(jnp.int32, (BLOCK, BLOCK), 0)
    high = lax.broadcasted_iota(jnp.int32, (BLOCK, BLOCK), 1)
    upper = jnp.where(low <= high, 1.0, 0.0).astype(F32)
    lower = jnp.where(low >= high, 1.0, 0.0).astype(F32)
    loads[0].wait()
    for b in range(BLOCKS):
        rates = rate[:, b * BLOCK:(b + 1) * BLOCK]
        run_row[b] = jnp.dot(
            rates, upper, preferred_element_type=F32, precision=lax.Precision.HIGHEST
        )
        run_col[b] = lax.dot_general(
            lower, rates, NT, preferred_element_type=F32, precision=lax.Precision.HIGHEST
        )
    loads[1].wait()
    loads[2].wait()
    for h in range(HEADS):
        state = jnp.zeros((HEAD_DIM, HEAD_DIM), F32)
        ahead = jnp.zeros((1, 1), F32)
        for b in range(BLOCKS):
            rows = slice(b * BLOCK, (b + 1) * BLOCK)
            run = run_col[b, :, h:h + 1]
            total = run[BLOCK - 1:BLOCK, :]
            start[b, h] = state
            lead[b, h] = jnp.broadcast_to(jnp.exp(ahead), (8, HEAD_DIM))
            keys = (k[rows, head_columns(h)].astype(F32) * jnp.exp(total - run)).astype(BF16)
            added = lax.dot_general(
                keys, v[rows, head_columns(h)], TN, preferred_element_type=F32
            )
            state = jnp.exp(total) * state + added
            ahead = ahead + total
        through = jnp.broadcast_to(jnp.exp(ahead), (per_head, 8, HEAD_DIM))
        pieces = pl.ds(h * per_head, per_head)
        state_send[pieces, 0:slice_rows, :] = state.reshape(per_head, slice_rows, HEAD_DIM)
        state_send[pieces, slice_rows:slice_rows + 8, :] = through

    pl.semaphore_wait(barrier, seq_size + 2)

    def slice_out(peer):
        return pltpu.make_async_remote_copy(
            src_ref=state_send.at[peer], dst_ref=state_recv.at[me],
            send_sem=a_send.at[peer], recv_sem=a_recv.at[me],
            device_id=(peer, head), device_id_type=MESH,
        )

    def slice_in(peer):
        return pltpu.make_async_remote_copy(
            src_ref=state_send.at[peer], dst_ref=state_recv.at[peer],
            send_sem=a_send.at[peer], recv_sem=a_recv.at[peer],
            device_id=(peer, head), device_id_type=MESH,
        )

    def scan_out(peer):
        return pltpu.make_async_remote_copy(
            src_ref=scan_send.at[peer], dst_ref=scan_recv.at[me],
            send_sem=b_send.at[peer], recv_sem=b_recv.at[me],
            device_id=(peer, head), device_id_type=MESH,
        )

    def scan_in(peer):
        return pltpu.make_async_remote_copy(
            src_ref=scan_send.at[peer], dst_ref=scan_recv.at[peer],
            send_sem=b_send.at[peer], recv_sem=b_recv.at[peer],
            device_id=(peer, head), device_id_type=MESH,
        )

    def send_slice(d, carry):
        slice_out(lax.rem(me + d, seq_size)).start()
        return carry

    lax.fori_loop(1, seq_size, send_slice, 0)
    state_recv[me] = state_send[me]

    loads[4].wait()
    pair_copies = []
    for i in range(PARTS):
        columns = slice(i * WIDE, (i + 1) * WIDE)
        w_send[i] = w[:, columns].astype(F32)
        pair_copies.append(
            pltpu.make_async_remote_copy(
                src_ref=w_send.at[i], dst_ref=w_recv.at[i],
                send_sem=w_ssem.at[i], recv_sem=w_rsem.at[i],
                device_id=(me, partner), device_id_type=MESH,
            )
        )
        pair_copies[-1].start()

    loads[3].wait()
    causal = low >= high

    def inside(b, carry):
        rows = pl.ds(pl.multiple_of(b * BLOCK, BLOCK), BLOCK)
        for h in range(HEADS):
            scores = lax.dot_general(
                q[rows, head_columns(h)], k[rows, head_columns(h)], NT,
                preferred_element_type=F32,
            )
            spread = run_col[b, :, h:h + 1] - run_row[b, h:h + 1, :]
            decay = jnp.exp(jnp.where(causal, spread, -1e30))
            weights = (scores * decay).astype(BF16)
            att[rows, head_columns(h)] = jnp.dot(
                weights, v[rows, head_columns(h)], preferred_element_type=F32
            )
        return carry

    lax.fori_loop(0, BLOCKS - 1, inside, 0)

    def arrive(d, carry):
        slice_in(lax.rem(me + d, seq_size)).wait_recv()
        return carry

    lax.fori_loop(1, seq_size, arrive, 0)

    def scan(p, state):
        scan_send[p] = state
        return state_recv[p, slice_rows:slice_rows + 1, :] * state + state_recv[p, 0:slice_rows, :]

    lax.fori_loop(0, seq_size, scan, jnp.zeros((slice_rows, HEAD_DIM), F32))

    def send_scan(d, carry):
        scan_out(lax.rem(me + d, seq_size)).start()
        return carry

    lax.fori_loop(1, seq_size, send_scan, 0)
    scan_recv[me] = scan_send[me]

    inside(BLOCKS - 1, 0)
    loads[5].wait()
    for i in range(PARTS):
        pair_copies[i].wait_recv()
        w_pair[:, i * WIDE:(i + 1) * WIDE] = w_recv[i].astype(BF16)

    def arrive_scan(d, carry):
        scan_in(lax.rem(me + d, seq_size)).wait_recv()
        return carry

    lax.fori_loop(1, seq_size, arrive_scan, 0)

    hid_copies = []

    def hide(t, b):
        rows = pl.ds(pl.multiple_of(b * BLOCK, BLOCK), BLOCK)
        for h in range(HEADS):
            incoming = scan_recv[h * per_head:(h + 1) * per_head].reshape(HEAD_DIM, HEAD_DIM)
            state = start[b, h] + lead[b, h, 0:1, :] * incoming
            top = state.astype(BF16)
            rest = (state - top.astype(F32)).astype(BF16)
            queries = q[rows, head_columns(h)]
            carried = jnp.dot(queries, top, preferred_element_type=F32) + jnp.dot(
                queries, rest, preferred_element_type=F32
            )
            attended = att[rows, head_columns(h)] + carried * jnp.exp(run_col[b, :, h:h + 1])
            mean = jnp.mean(attended * attended, axis=-1, keepdims=True)
            gate = g[rows, head_columns(h)].astype(F32)
            gated = attended * lax.rsqrt(mean + 1e-6) * (gate / (1.0 + jnp.exp(-gate)))
            hid[t, :, :, head_columns(h)] = gated.astype(BF16).astype(F32).reshape(
                2, HALF, HEAD_DIM
            )
        copy = pltpu.make_async_remote_copy(
            src_ref=hid.at[t, 1 - core], dst_ref=hid_recv.at[t],
            send_sem=h_ssem.at[t], recv_sem=h_rsem.at[t],
            device_id=(me, partner), device_id_type=MESH,
        )
        copy.start()
        hid_copies.append(copy)

    def project(t, n):
        columns = slice(n * CHUNK, (n + 1) * CHUNK)
        return jnp.dot(
            hid[t, core].astype(BF16), w[:, columns], preferred_element_type=F32
        ) + jnp.dot(hid_recv[t].astype(BF16), w_pair[:, columns], preferred_element_type=F32)

    def across(kind, n, src, dst, other):
        return pltpu.make_async_remote_copy(
            src_ref=src, dst_ref=dst, send_sem=y_send.at[kind, n], recv_sem=y_recv.at[kind, n],
            device_id=(me, other), device_id_type=MESH,
        )

    blocks = [lax.rem(row + 2, 4), lax.rem(row + 1, 4), lax.rem(row + 3, 4), row]
    far_copies = [
        across(0, n, far.at[n], far_recv.at[n], up if n < SIDE else down) for n in range(CHUNKS)
    ]
    direct_copies = [
        across(
            1, n, minus.at[n] if n < SIDE else plus.at[n], direct_recv.at[n],
            down if n < SIDE else up,
        )
        for n in range(CHUNKS)
    ]
    sum_copies = [
        across(
            2, n, plus.at[n] if n < SIDE else minus.at[n], sum_recv.at[n],
            up if n < SIDE else down,
        )
        for n in range(CHUNKS)
    ]
    order = [n // 2 + (n % 2) * SIDE for n in range(CHUNKS)]

    hide(0, blocks[0])
    hide(1, blocks[1])
    hid_copies[0].wait_recv()
    for n in order:
        far[n] = project(0, n)
        far_copies[n].start()
    hide(2, blocks[2])
    hid_copies[1].wait_recv()
    for n in range(SIDE, CHUNKS):
        plus[n] = project(1, n)
        direct_copies[n].start()
    hid_copies[2].wait_recv()
    for n in range(SIDE):
        minus[n] = project(2, n)
        direct_copies[n].start()
    for n in range(SIDE):
        plus[n] = project(1, n)
        minus[SIDE + n] = project(2, SIDE + n)
        far_copies[n].wait_recv()
        plus[n] += far_recv[n]
        sum_copies[n].start()
        far_copies[SIDE + n].wait_recv()
        minus[SIDE + n] += far_recv[SIDE + n]
        sum_copies[SIDE + n].start()
    hide(3, blocks[3])
    hid_copies[3].wait_recv()
    for n in order:
        own[n] = project(3, n)
    for n in order:
        direct_copies[n].wait_recv()
        own[n] += direct_recv[n]
    for n in order:
        sum_copies[n].wait_recv()
        out_ref[:, n * CHUNK:(n + 1) * CHUNK] = (own[n] + sum_recv[n]).astype(BF16)

    def settle(d, carry):
        peer = lax.rem(me + d, seq_size)
        slice_out(peer).wait_send()
        scan_out(peer).wait_send()
        return carry

    lax.fori_loop(1, seq_size, settle, 0)
    for copy in pair_copies + hid_copies + far_copies + direct_copies + sum_copies:
        copy.wait_send()


def per_device(seq_size, queries, key_vectors, value_vectors, gate_input, log_decay, out_weight):
    tokens = BLOCKS * BLOCK
    slice_rows = FEATURES // seq_size
    whole = pl.BlockSpec(memory_space=pl.ANY)
    dma = pltpu.SemaphoreType.DMA
    vmem = pltpu.VMEM
    return pl.pallas_call(
        functools.partial(kernel, seq_size),
        out_shape=jax.ShapeDtypeStruct((HALF, WIDTH), BF16),
        in_specs=[whole] * 6,
        out_specs=pl.BlockSpec(memory_space=pltpu.VMEM),
        scratch_shapes=[
            vmem((HEADS, tokens), F32),
            vmem((tokens, FEATURES), BF16),
            vmem((tokens, FEATURES), BF16),
            vmem((tokens, FEATURES), BF16),
            vmem((tokens, FEATURES), BF16),
            vmem((FEATURES, WIDTH), BF16),
            vmem((PARTS, FEATURES, WIDE), F32),
            vmem((PARTS, FEATURES, WIDE), F32),
            vmem((FEATURES, WIDTH), BF16),
            vmem((BLOCKS, BLOCK, HEADS), F32),
            vmem((BLOCKS, HEADS, BLOCK), F32),
            vmem((BLOCKS, HEADS, HEAD_DIM, HEAD_DIM), F32),
            vmem((BLOCKS, HEADS, 8, HEAD_DIM), F32),
            vmem((seq_size, slice_rows + 8, HEAD_DIM), F32),
            vmem((seq_size, slice_rows + 8, HEAD_DIM), F32),
            vmem((seq_size, slice_rows, HEAD_DIM), F32),
            vmem((seq_size, slice_rows, HEAD_DIM), F32),
            vmem((tokens, FEATURES), F32),
            vmem((BLOCKS, 2, HALF, FEATURES), F32),
            vmem((BLOCKS, HALF, FEATURES), F32),
            vmem((CHUNKS, HALF, CHUNK), F32),
            vmem((CHUNKS, HALF, CHUNK), F32),
            vmem((CHUNKS, HALF, CHUNK), F32),
            vmem((CHUNKS, HALF, CHUNK), F32),
            vmem((CHUNKS, HALF, CHUNK), F32),
            vmem((CHUNKS, HALF, CHUNK), F32),
            vmem((CHUNKS, HALF, CHUNK), F32),
            dma((6,)),
            dma((seq_size,)), dma((seq_size,)), dma((seq_size,)), dma((seq_size,)),
            dma((PARTS,)), dma((PARTS,)), dma((BLOCKS,)), dma((BLOCKS,)),
            dma((3, CHUNKS)), dma((3, CHUNKS)),
        ],
        compiler_params=pltpu.CompilerParams(
            collective_id=0, has_side_effects=True, vmem_limit_bytes=62 * 1024 * 1024
        ),
    )(log_decay.T, key_vectors, value_vectors, queries, gate_input, out_weight)


def solution(mesh):
    placed = (
        P("seq", "head"),
        P("seq", "head"),
        P("seq", "head"),
        P("seq", "head"),
        P("seq", "head"),
        P("head", None),
    )
    return jax.shard_map(
        functools.partial(per_device, mesh.shape["seq"]),
        mesh=mesh, in_specs=placed, out_specs=P(("seq", "head"), None), check_vma=False,
    )
```

```python
import functools

import jax
import jax.numpy as jnp
from jax import lax
from jax.experimental import pallas as pl
from jax.experimental.pallas import tpu as pltpu
from jax.sharding import PartitionSpec as P

HEAD_DIM = 128
BLOCK = 256
HALF = 128
HEADS = 4
BLOCKS = 4
FEATURES = HEADS * HEAD_DIM
WIDTH = 4096
CHUNK = 512
CHUNKS = WIDTH // CHUNK
SIDE = CHUNKS // 2
F32 = jnp.float32
BF16 = jnp.bfloat16
MESH = pl.DeviceIdType.MESH
NT = (((1,), (1,)), ((), ()))
TN = (((0,), (0,)), ((), ()))


def head_columns(h):
    return slice(h * HEAD_DIM, (h + 1) * HEAD_DIM)


def kernel(
    seq_size, rate_hbm, k_hbm, v_hbm, q_hbm, g_hbm, w_hbm, out_ref,
    rate, padded, k, v, q, g, w, w_send, w_recv, w_pair,
    run_col, run_row, start, lead, state_send, state_recv, scan_send, scan_recv,
    att, since, silu, entry, hid, hid_recv, far, plus, minus, own, far_recv, direct_recv,
    sum_recv, result,
    load_sem, a_send, a_recv, w_ssem, w_rsem, h_ssem, h_rsem,
    y_send, y_recv, o_sem,
):
    me = lax.axis_index("seq")
    head = lax.axis_index("head")
    row = head // 2
    core = lax.rem(head, 2)
    partner = row * 2 + (1 - core)
    up = lax.rem(row + 1, 4) * 2 + core
    down = lax.rem(row + 3, 4) * 2 + core
    slice_rows = FEATURES // seq_size
    per_head = HEAD_DIM // slice_rows

    loads = [
        pltpu.make_async_copy(src, dst, load_sem.at[i])
        for i, (src, dst) in enumerate(
            ((rate_hbm, rate), (k_hbm, k), (v_hbm, v), (q_hbm, q), (w_hbm, w), (g_hbm, g))
        )
    ]
    for load in loads:
        load.start()

    barrier = pltpu.get_barrier_semaphore()

    def greet(d, carry):
        peer = lax.rem(me + d, seq_size)
        pl.semaphore_signal(barrier, inc=1, device_id=(peer, head), device_id_type=MESH)
        return carry

    lax.fori_loop(1, seq_size, greet, 0)
    for other in (partner, up, down):
        pl.semaphore_signal(barrier, inc=1, device_id=(me, other), device_id_type=MESH)

    low = lax.broadcasted_iota(jnp.int32, (BLOCK, BLOCK), 0)
    high = lax.broadcasted_iota(jnp.int32, (BLOCK, BLOCK), 1)
    upper = jnp.where(low <= high, 1.0, 0.0).astype(BF16)
    lower = jnp.where(low >= high, 1.0, 0.0).astype(BF16)
    loads[0].wait()
    for b in range(BLOCKS):
        padded[b, 0:HEADS, :] = rate[:, b * BLOCK:(b + 1) * BLOCK]
        padded[b, HEADS:8, :] = jnp.zeros((8 - HEADS, BLOCK), F32)
    rates = padded[...].reshape(BLOCKS * 8, BLOCK)
    run_rows = jnp.zeros((BLOCKS * 8, BLOCK), F32)
    run_cols = jnp.zeros((BLOCK, BLOCKS * 8), F32)
    for _ in range(3):
        piece = rates.astype(BF16)
        run_rows += jnp.dot(piece, upper, preferred_element_type=F32)
        run_cols += lax.dot_general(lower, piece, NT, preferred_element_type=F32)
        rates = rates - piece.astype(F32)
    run_row[...] = run_rows.reshape(BLOCKS, 8, BLOCK)
    for b in range(BLOCKS):
        run_col[b] = run_cols[:, 8 * b:8 * b + 8]
    totals = run_rows[:, BLOCK - 1:BLOCK]
    key_scale = jnp.exp(totals - run_rows)
    block_decay = jnp.broadcast_to(jnp.exp(totals), (BLOCKS * 8, HEAD_DIM))
    ahead = jnp.zeros((8, 1), F32)
    for b in range(BLOCKS):
        lead[b] = jnp.broadcast_to(jnp.exp(ahead), (8, HEAD_DIM))
        ahead = ahead + totals[8 * b:8 * b + 8]
    through = jnp.broadcast_to(jnp.exp(ahead), (8, HEAD_DIM))
    loads[1].wait()
    loads[2].wait()
    for h in range(HEADS):
        state = jnp.zeros((HEAD_DIM, HEAD_DIM), F32)
        for b in range(BLOCKS):
            rows = slice(b * BLOCK, (b + 1) * BLOCK)
            line = slice(8 * b + h, 8 * b + h + 1)
            start[b, h] = state
            keys = (k[rows, head_columns(h)].T.astype(F32) * key_scale[line]).astype(BF16)
            added = jnp.dot(keys, v[rows, head_columns(h)], preferred_element_type=F32)
            state = block_decay[line] * state + added
        pieces = pl.ds(h * per_head, per_head)
        state_send[pieces, 0:slice_rows, :] = state.reshape(per_head, slice_rows, HEAD_DIM)
        state_send[pieces, slice_rows:slice_rows + 8, :] = jnp.broadcast_to(
            through[h:h + 1], (per_head, 8, HEAD_DIM)
        )

    pl.semaphore_wait(barrier, seq_size + 2)

    def exchange(phase, src, dst, peer):
        return pltpu.make_async_remote_copy(
            src_ref=src, dst_ref=dst, send_sem=a_send.at[phase], recv_sem=a_recv.at[phase],
            device_id=(peer, head), device_id_type=MESH,
        )

    others = pl.ds(0, seq_size - 1)
    next_peer = lax.rem(me + 1, seq_size)
    all_slices = exchange(0, state_send.at[others], state_recv.at[others], next_peer)
    all_scans = exchange(1, scan_send.at[others], scan_recv.at[others], next_peer)

    def send_slice(d, carry):
        peer = lax.rem(me + d, seq_size)
        exchange(0, state_send.at[peer], state_recv.at[me], peer).start()
        return carry

    lax.fori_loop(1, seq_size, send_slice, 0)
    state_recv[me] = state_send[me]

    blocks = [lax.rem(row + 2, 4), lax.rem(row + 1, 4), lax.rem(row + 3, 4), row]
    order = [n // 2 + (n % 2) * SIDE for n in range(CHUNKS)]

    def columns(n):
        return slice(n * CHUNK, (n + 1) * CHUNK)

    loads[4].wait()
    pair_copies = {}
    for n in order:
        w_send[n] = w[:, columns(n)].astype(F32)
        pair_copies[n] = pltpu.make_async_remote_copy(
            src_ref=w_send.at[n], dst_ref=w_recv.at[n],
            send_sem=w_ssem.at[n], recv_sem=w_rsem.at[n],
            device_id=(me, partner), device_id_type=MESH,
        )
        pair_copies[n].start()

    def receive_weights(n):
        pair_copies[n].wait_recv()
        w_pair[:, columns(n)] = w_recv[n].astype(BF16)

    loads[3].wait()
    loads[5].wait()
    causal = low >= high

    def inside(b):
        rows = pl.ds(pl.multiple_of(b * BLOCK, BLOCK), BLOCK)
        for h in range(HEADS):
            scores = lax.dot_general(
                q[rows, head_columns(h)], k[rows, head_columns(h)], NT,
                preferred_element_type=F32,
            )
            run = run_col[b, :, h:h + 1]
            decay = jnp.exp(jnp.where(causal, run - run_row[b, h:h + 1, :], -1e30))
            weights = (scores * decay).astype(BF16)
            att[rows, head_columns(h)] = jnp.dot(
                weights, v[rows, head_columns(h)], preferred_element_type=F32
            )
            since[rows, head_columns(h)] = jnp.broadcast_to(jnp.exp(run), (BLOCK, HEAD_DIM))
            gate = g[rows, head_columns(h)].astype(F32)
            silu[rows, head_columns(h)] = gate / (1.0 + jnp.exp(-gate))

    inside(blocks[0])
    inside(blocks[1])

    all_slices.wait_recv()

    def scan(p, state):
        scan_send[p] = state
        return state_recv[p, slice_rows:slice_rows + 1, :] * state + state_recv[p, 0:slice_rows, :]

    lax.fori_loop(0, seq_size, scan, jnp.zeros((slice_rows, HEAD_DIM), F32), unroll=4)

    def send_scan(d, carry):
        peer = lax.rem(me + d, seq_size)
        exchange(1, scan_send.at[peer], scan_recv.at[me], peer).start()
        return carry

    lax.fori_loop(1, seq_size, send_scan, 0)
    scan_recv[me] = scan_send[me]

    inside(blocks[2])
    inside(blocks[3])
    for n in order[:SIDE]:
        receive_weights(n)
    all_scans.wait_recv()

    hid_copies = []

    def hide(t):
        b = blocks[t]
        for h in range(HEADS):
            incoming = scan_recv[h * per_head:(h + 1) * per_head].reshape(HEAD_DIM, HEAD_DIM)
            state = start[b, h] + lead[b, h:h + 1, :] * incoming
            top = state.astype(BF16)
            entry[0, h] = top
            entry[1, h] = (state - top.astype(F32)).astype(BF16)
        for side in (1 - core, core):
            rows = pl.ds(pl.multiple_of(b * BLOCK + side * HALF, HALF), HALF)
            for h in range(HEADS):
                queries = q[rows, head_columns(h)]
                carried = jnp.dot(queries, entry[0, h], preferred_element_type=F32) + jnp.dot(
                    queries, entry[1, h], preferred_element_type=F32
                )
                attended = att[rows, head_columns(h)] + carried * since[rows, head_columns(h)]
                mean = jnp.mean(attended * attended, axis=-1, keepdims=True)
                gated = attended * lax.rsqrt(mean + 1e-6) * silu[rows, head_columns(h)]
                hid[t, side, :, head_columns(h)] = gated.astype(BF16).astype(F32)
            if side is not core:
                copy = pltpu.make_async_remote_copy(
                    src_ref=hid.at[t, 1 - core], dst_ref=hid_recv.at[t],
                    send_sem=h_ssem.at[t], recv_sem=h_rsem.at[t],
                    device_id=(me, partner), device_id_type=MESH,
                )
                copy.start()
                hid_copies.append(copy)

    def project(t, n):
        return jnp.dot(
            hid[t, core].astype(BF16), w[:, columns(n)], preferred_element_type=F32
        ) + jnp.dot(hid_recv[t].astype(BF16), w_pair[:, columns(n)], preferred_element_type=F32)

    def across(kind, n, src, dst, other):
        return pltpu.make_async_remote_copy(
            src_ref=src, dst_ref=dst, send_sem=y_send.at[kind, n], recv_sem=y_recv.at[kind, n],
            device_id=(me, other), device_id_type=MESH,
        )

    far_copies = [
        across(0, n, far.at[n], far_recv.at[n], up if n < SIDE else down) for n in range(CHUNKS)
    ]
    direct_copies = [
        across(
            1, n, minus.at[n] if n < SIDE else plus.at[n], direct_recv.at[n],
            down if n < SIDE else up,
        )
        for n in range(CHUNKS)
    ]
    sum_copies = [
        across(
            2, n, plus.at[n] if n < SIDE else minus.at[n], sum_recv.at[n],
            up if n < SIDE else down,
        )
        for n in range(CHUNKS)
    ]

    hide(0)
    hid_copies[0].wait_recv()
    for i, n in enumerate(order):
        if i >= SIDE:
            receive_weights(n)
        far[n] = project(0, n)
        far_copies[n].start()
    hide(1)
    hide(2)
    hid_copies[1].wait_recv()
    for n in range(SIDE, CHUNKS):
        plus[n] = project(1, n)
        direct_copies[n].start()
    hid_copies[2].wait_recv()
    for n in range(SIDE):
        minus[n] = project(2, n)
        direct_copies[n].start()
    for n in range(SIDE):
        plus[n] = project(1, n)
        minus[SIDE + n] = project(2, SIDE + n)
        far_copies[n].wait_recv()
        plus[n] += far_recv[n]
        sum_copies[n].start()
        far_copies[SIDE + n].wait_recv()
        minus[SIDE + n] += far_recv[SIDE + n]
        sum_copies[SIDE + n].start()
    hide(3)
    hid_copies[3].wait_recv()
    for n in order:
        own[n] = project(3, n)
    for n in order:
        direct_copies[n].wait_recv()
        own[n] += direct_recv[n]
    out_copies = []
    for n in order:
        sum_copies[n].wait_recv()
        result[:, columns(n)] = (own[n] + sum_recv[n]).astype(BF16)
        out_copies.append(
            pltpu.make_async_copy(
                result.at[:, columns(n)], out_ref.at[:, columns(n)], o_sem.at[n]
            )
        )
        out_copies[-1].start()

    all_slices.wait_send()
    all_scans.wait_send()
    for copy in list(pair_copies.values()) + hid_copies + far_copies + direct_copies + sum_copies:
        copy.wait_send()
    for copy in out_copies:
        copy.wait()


def per_device(seq_size, queries, key_vectors, value_vectors, gate_input, log_decay, out_weight):
    tokens = BLOCKS * BLOCK
    slice_rows = FEATURES // seq_size
    whole = pl.BlockSpec(memory_space=pl.ANY)
    dma = pltpu.SemaphoreType.DMA
    vmem = pltpu.VMEM
    return pl.pallas_call(
        functools.partial(kernel, seq_size),
        out_shape=jax.ShapeDtypeStruct((HALF, WIDTH), BF16),
        in_specs=[whole] * 6,
        out_specs=whole,
        scratch_shapes=[
            vmem((HEADS, tokens), F32),
            vmem((BLOCKS, 8, BLOCK), F32),
            vmem((tokens, FEATURES), BF16),
            vmem((tokens, FEATURES), BF16),
            vmem((tokens, FEATURES), BF16),
            vmem((tokens, FEATURES), BF16),
            vmem((FEATURES, WIDTH), BF16),
            vmem((CHUNKS, FEATURES, CHUNK), F32),
            vmem((CHUNKS, FEATURES, CHUNK), F32),
            vmem((FEATURES, WIDTH), BF16),
            vmem((BLOCKS, BLOCK, 8), F32),
            vmem((BLOCKS, 8, BLOCK), F32),
            vmem((BLOCKS, HEADS, HEAD_DIM, HEAD_DIM), F32),
            vmem((BLOCKS, 8, HEAD_DIM), F32),
            vmem((seq_size, slice_rows + 8, HEAD_DIM), F32),
            vmem((seq_size, slice_rows + 8, HEAD_DIM), F32),
            vmem((seq_size, slice_rows, HEAD_DIM), F32),
            vmem((seq_size, slice_rows, HEAD_DIM), F32),
            vmem((tokens, FEATURES), F32),
            vmem((tokens, FEATURES), F32),
            vmem((tokens, FEATURES), F32),
            vmem((2, HEADS, HEAD_DIM, HEAD_DIM), BF16),
            vmem((BLOCKS, 2, HALF, FEATURES), F32),
            vmem((BLOCKS, HALF, FEATURES), F32),
            vmem((CHUNKS, HALF, CHUNK), F32),
            vmem((CHUNKS, HALF, CHUNK), F32),
            vmem((CHUNKS, HALF, CHUNK), F32),
            vmem((CHUNKS, HALF, CHUNK), F32),
            vmem((CHUNKS, HALF, CHUNK), F32),
            vmem((CHUNKS, HALF, CHUNK), F32),
            vmem((CHUNKS, HALF, CHUNK), F32),
            vmem((HALF, WIDTH), BF16),
            dma((6,)), dma((2,)), dma((2,)), dma((CHUNKS,)), dma((CHUNKS,)), dma((BLOCKS,)), dma((BLOCKS,)),
            dma((3, CHUNKS)), dma((3, CHUNKS)), dma((CHUNKS,)),
        ],
        compiler_params=pltpu.CompilerParams(
            collective_id=0, has_side_effects=True, vmem_limit_bytes=62 * 1024 * 1024
        ),
    )(log_decay.T, key_vectors, value_vectors, queries, gate_input, out_weight)


def solution(mesh):
    placed = (
        P("seq", "head"),
        P("seq", "head"),
        P("seq", "head"),
        P("seq", "head"),
        P("seq", "head"),
        P("head", None),
    )
    return jax.shard_map(
        functools.partial(per_device, mesh.shape["seq"]),
        mesh=mesh, in_specs=placed, out_specs=P(("seq", "head"), None), check_vma=False,
    )
```

```python
import functools

import jax
import jax.numpy as jnp
from jax import lax
from jax.experimental import pallas as pl
from jax.experimental.pallas import tpu as pltpu
from jax.sharding import PartitionSpec as P

HEAD_DIM = 128
BLOCK = 256
HALF = 128
HEADS = 4
BLOCKS = 4
FEATURES = HEADS * HEAD_DIM
WIDTH = 4096
CHUNK = 512
CHUNKS = WIDTH // CHUNK
SIDE = CHUNKS // 2
F32 = jnp.float32
BF16 = jnp.bfloat16
MESH = pl.DeviceIdType.MESH
NT = (((1,), (1,)), ((), ()))
TN = (((0,), (0,)), ((), ()))


def head_columns(h):
    return slice(h * HEAD_DIM, (h + 1) * HEAD_DIM)


def kernel(
    seq_size, rate_hbm, k_hbm, v_hbm, q_hbm, g_hbm, w_hbm, out_ref,
    rate, padded, k, v, q, g, w, w_send, w_recv, w_pair,
    run_col, run_row, start, lead, state_send, state_recv, scan_send, scan_recv,
    att, since, silu, entry, hid, hid_recv, far, plus, minus, own, far_recv, direct_recv,
    sum_recv, result,
    load_sem, a_send, a_recv, w_ssem, w_rsem, h_ssem, h_rsem,
    y_send, y_recv, o_sem,
):
    me = lax.axis_index("seq")
    head = lax.axis_index("head")
    row = head // 2
    core = lax.rem(head, 2)
    partner = row * 2 + (1 - core)
    up = lax.rem(row + 1, 4) * 2 + core
    down = lax.rem(row + 3, 4) * 2 + core
    slice_rows = FEATURES // seq_size
    per_head = HEAD_DIM // slice_rows

    loads = [
        pltpu.make_async_copy(src, dst, load_sem.at[i])
        for i, (src, dst) in enumerate(
            ((rate_hbm, rate), (k_hbm, k), (v_hbm, v), (q_hbm, q), (w_hbm, w), (g_hbm, g))
        )
    ]
    for load in loads[:3]:
        load.start()

    barrier = pltpu.get_barrier_semaphore()

    def greet(d, carry):
        peer = lax.rem(me + d, seq_size)
        pl.semaphore_signal(barrier, inc=1, device_id=(peer, head), device_id_type=MESH)
        return carry

    lax.fori_loop(1, seq_size, greet, 0)
    for other in (partner, up, down):
        pl.semaphore_signal(barrier, inc=1, device_id=(me, other), device_id_type=MESH)

    low = lax.broadcasted_iota(jnp.int32, (BLOCK, BLOCK), 0)
    high = lax.broadcasted_iota(jnp.int32, (BLOCK, BLOCK), 1)
    upper = jnp.where(low <= high, 1.0, 0.0).astype(BF16)
    lower = jnp.where(low >= high, 1.0, 0.0).astype(BF16)
    loads[0].wait()
    for b in range(BLOCKS):
        padded[b, 0:HEADS, :] = rate[:, b * BLOCK:(b + 1) * BLOCK]
        padded[b, HEADS:8, :] = jnp.zeros((8 - HEADS, BLOCK), F32)
    rates = padded[...].reshape(BLOCKS * 8, BLOCK)
    run_rows = jnp.zeros((BLOCKS * 8, BLOCK), F32)
    run_cols = jnp.zeros((BLOCK, BLOCKS * 8), F32)
    for _ in range(3):
        piece = rates.astype(BF16)
        run_rows += jnp.dot(piece, upper, preferred_element_type=F32)
        run_cols += lax.dot_general(lower, piece, NT, preferred_element_type=F32)
        rates = rates - piece.astype(F32)
    run_row[...] = run_rows.reshape(BLOCKS, 8, BLOCK)
    for b in range(BLOCKS):
        run_col[b] = run_cols[:, 8 * b:8 * b + 8]
    totals = run_rows[:, BLOCK - 1:BLOCK]
    key_scale = jnp.exp(totals - run_rows)
    block_decay = jnp.broadcast_to(jnp.exp(totals), (BLOCKS * 8, HEAD_DIM))
    ahead = jnp.zeros((8, 1), F32)
    for b in range(BLOCKS):
        lead[b] = jnp.broadcast_to(jnp.exp(ahead), (8, HEAD_DIM))
        ahead = ahead + totals[8 * b:8 * b + 8]
    through = jnp.broadcast_to(jnp.exp(ahead), (8, HEAD_DIM))
    loads[1].wait()
    loads[2].wait()
    for load in loads[3:]:
        load.start()
    for h in range(HEADS):
        state = jnp.zeros((HEAD_DIM, HEAD_DIM), F32)
        for b in range(BLOCKS):
            rows = slice(b * BLOCK, (b + 1) * BLOCK)
            line = slice(8 * b + h, 8 * b + h + 1)
            start[b, h] = state
            keys = (k[rows, head_columns(h)].T.astype(F32) * key_scale[line]).astype(BF16)
            added = jnp.dot(keys, v[rows, head_columns(h)], preferred_element_type=F32)
            state = block_decay[line] * state + added
        pieces = pl.ds(h * per_head, per_head)
        state_send[pieces, 0:slice_rows, :] = state.reshape(per_head, slice_rows, HEAD_DIM)
        state_send[pieces, slice_rows:slice_rows + 8, :] = jnp.broadcast_to(
            through[h:h + 1], (per_head, 8, HEAD_DIM)
        )

    pl.semaphore_wait(barrier, seq_size + 2)

    def exchange(phase, src, dst, peer):
        return pltpu.make_async_remote_copy(
            src_ref=src, dst_ref=dst, send_sem=a_send.at[phase], recv_sem=a_recv.at[phase],
            device_id=(peer, head), device_id_type=MESH,
        )

    others = pl.ds(0, seq_size - 1)
    next_peer = lax.rem(me + 1, seq_size)
    message = pl.ds(0, slice_rows + 1)
    all_slices = exchange(
        0, state_send.at[others, message], state_recv.at[others, message], next_peer
    )
    all_scans = exchange(1, scan_send.at[others], scan_recv.at[others], next_peer)

    def each_peer(send):
        send(lax.rem(me + seq_size // 2, seq_size))

        def both_ways(d, carry):
            send(lax.rem(me + seq_size // 2 + d, seq_size))
            send(lax.rem(me + seq_size // 2 - d, seq_size))
            return carry

        lax.fori_loop(1, seq_size // 2, both_ways, 0)

    def send_slice(peer):
        exchange(0, state_send.at[peer, message], state_recv.at[me, message], peer).start()

    each_peer(send_slice)
    state_recv[me] = state_send[me]

    blocks = [lax.rem(row + 2, 4), lax.rem(row + 1, 4), lax.rem(row + 3, 4), row]
    order = [n // 2 + (n % 2) * SIDE for n in range(CHUNKS)]

    def columns(n):
        return slice(n * CHUNK, (n + 1) * CHUNK)

    loads[4].wait()
    pair_copies = {}
    for n in order:
        w_send[n] = w[:, columns(n)].astype(F32)
        pair_copies[n] = pltpu.make_async_remote_copy(
            src_ref=w_send.at[n], dst_ref=w_recv.at[n],
            send_sem=w_ssem.at[n], recv_sem=w_rsem.at[n],
            device_id=(me, partner), device_id_type=MESH,
        )
        pair_copies[n].start()

    def receive_weights(n):
        pair_copies[n].wait_recv()
        w_pair[:, columns(n)] = w_recv[n].astype(BF16)

    loads[3].wait()
    loads[5].wait()
    causal = low >= high

    def inside(b):
        rows = pl.ds(pl.multiple_of(b * BLOCK, BLOCK), BLOCK)
        for h in range(HEADS):
            scores = lax.dot_general(
                q[rows, head_columns(h)], k[rows, head_columns(h)], NT,
                preferred_element_type=F32,
            )
            run = run_col[b, :, h:h + 1]
            decay = jnp.exp(jnp.where(causal, run - run_row[b, h:h + 1, :], -1e30))
            weights = (scores * decay).astype(BF16)
            att[rows, head_columns(h)] = jnp.dot(
                weights, v[rows, head_columns(h)], preferred_element_type=F32
            )
            since[rows, head_columns(h)] = jnp.broadcast_to(jnp.exp(run), (BLOCK, HEAD_DIM))
            gate = g[rows, head_columns(h)].astype(F32)
            silu[rows, head_columns(h)] = gate / (1.0 + jnp.exp(-gate))

    inside(blocks[0])
    inside(blocks[1])

    all_slices.wait_recv()

    def scan(p, state):
        scan_send[p] = state
        return state_recv[p, slice_rows:slice_rows + 1, :] * state + state_recv[p, 0:slice_rows, :]

    lax.fori_loop(0, seq_size, scan, jnp.zeros((slice_rows, HEAD_DIM), F32), unroll=4)

    def send_scan(peer):
        exchange(1, scan_send.at[peer], scan_recv.at[me], peer).start()

    each_peer(send_scan)
    scan_recv[me] = scan_send[me]

    inside(blocks[2])
    inside(blocks[3])
    for n in order[:SIDE]:
        receive_weights(n)
    all_scans.wait_recv()

    hid_copies = []

    def hide(t):
        b = blocks[t]
        for h in range(HEADS):
            incoming = scan_recv[h * per_head:(h + 1) * per_head].reshape(HEAD_DIM, HEAD_DIM)
            state = start[b, h] + lead[b, h:h + 1, :] * incoming
            top = state.astype(BF16)
            entry[0, h] = top
            entry[1, h] = (state - top.astype(F32)).astype(BF16)
        for side in (1 - core, core):
            rows = pl.ds(pl.multiple_of(b * BLOCK + side * HALF, HALF), HALF)
            for h in range(HEADS):
                queries = q[rows, head_columns(h)]
                carried = jnp.dot(queries, entry[0, h], preferred_element_type=F32) + jnp.dot(
                    queries, entry[1, h], preferred_element_type=F32
                )
                attended = att[rows, head_columns(h)] + carried * since[rows, head_columns(h)]
                mean = jnp.mean(attended * attended, axis=-1, keepdims=True)
                gated = attended * lax.rsqrt(mean + 1e-6) * silu[rows, head_columns(h)]
                hid[t, side, :, head_columns(h)] = gated.astype(BF16).astype(F32)
            if side is not core:
                copy = pltpu.make_async_remote_copy(
                    src_ref=hid.at[t, 1 - core], dst_ref=hid_recv.at[t],
                    send_sem=h_ssem.at[t], recv_sem=h_rsem.at[t],
                    device_id=(me, partner), device_id_type=MESH,
                )
                copy.start()
                hid_copies.append(copy)

    def project(t, n):
        return jnp.dot(
            hid[t, core].astype(BF16), w[:, columns(n)], preferred_element_type=F32
        ) + jnp.dot(hid_recv[t].astype(BF16), w_pair[:, columns(n)], preferred_element_type=F32)

    def across(kind, n, src, dst, other):
        return pltpu.make_async_remote_copy(
            src_ref=src, dst_ref=dst, send_sem=y_send.at[kind, n], recv_sem=y_recv.at[kind, n],
            device_id=(me, other), device_id_type=MESH,
        )

    far_copies = [
        across(0, n, far.at[n], far_recv.at[n], up if n < SIDE else down) for n in range(CHUNKS)
    ]
    direct_copies = [
        across(
            1, n, minus.at[n] if n < SIDE else plus.at[n], direct_recv.at[n],
            down if n < SIDE else up,
        )
        for n in range(CHUNKS)
    ]
    sum_copies = [
        across(
            2, n, plus.at[n] if n < SIDE else minus.at[n], sum_recv.at[n],
            up if n < SIDE else down,
        )
        for n in range(CHUNKS)
    ]

    hide(0)
    hid_copies[0].wait_recv()
    for i, n in enumerate(order):
        if i >= SIDE:
            receive_weights(n)
        far[n] = project(0, n)
        far_copies[n].start()
    hide(1)
    hide(2)
    hid_copies[1].wait_recv()
    for n in range(SIDE, CHUNKS):
        plus[n] = project(1, n)
        direct_copies[n].start()
    hid_copies[2].wait_recv()
    for n in range(SIDE):
        minus[n] = project(2, n)
        direct_copies[n].start()
    for n in range(SIDE):
        plus[n] = project(1, n)
        minus[SIDE + n] = project(2, SIDE + n)
        far_copies[n].wait_recv()
        plus[n] += far_recv[n]
        sum_copies[n].start()
        far_copies[SIDE + n].wait_recv()
        minus[SIDE + n] += far_recv[SIDE + n]
        sum_copies[SIDE + n].start()
    hide(3)
    hid_copies[3].wait_recv()
    for n in order:
        own[n] = project(3, n)
    for n in order:
        direct_copies[n].wait_recv()
        own[n] += direct_recv[n]
    out_copies = []
    for n in order:
        sum_copies[n].wait_recv()
        result[:, columns(n)] = (own[n] + sum_recv[n]).astype(BF16)
        out_copies.append(
            pltpu.make_async_copy(
                result.at[:, columns(n)], out_ref.at[:, columns(n)], o_sem.at[n]
            )
        )
        out_copies[-1].start()

    all_slices.wait_send()
    all_scans.wait_send()
    for copy in list(pair_copies.values()) + hid_copies + far_copies + direct_copies + sum_copies:
        copy.wait_send()
    for copy in out_copies:
        copy.wait()


def per_device(seq_size, queries, key_vectors, value_vectors, gate_input, log_decay, out_weight):
    tokens = BLOCKS * BLOCK
    slice_rows = FEATURES // seq_size
    whole = pl.BlockSpec(memory_space=pl.ANY)
    dma = pltpu.SemaphoreType.DMA
    vmem = pltpu.VMEM
    return pl.pallas_call(
        functools.partial(kernel, seq_size),
        out_shape=jax.ShapeDtypeStruct((HALF, WIDTH), BF16),
        in_specs=[whole] * 6,
        out_specs=whole,
        scratch_shapes=[
            vmem((HEADS, tokens), F32),
            vmem((BLOCKS, 8, BLOCK), F32),
            vmem((tokens, FEATURES), BF16),
            vmem((tokens, FEATURES), BF16),
            vmem((tokens, FEATURES), BF16),
            vmem((tokens, FEATURES), BF16),
            vmem((FEATURES, WIDTH), BF16),
            vmem((CHUNKS, FEATURES, CHUNK), F32),
            vmem((CHUNKS, FEATURES, CHUNK), F32),
            vmem((FEATURES, WIDTH), BF16),
            vmem((BLOCKS, BLOCK, 8), F32),
            vmem((BLOCKS, 8, BLOCK), F32),
            vmem((BLOCKS, HEADS, HEAD_DIM, HEAD_DIM), F32),
            vmem((BLOCKS, 8, HEAD_DIM), F32),
            vmem((seq_size, slice_rows + 8, HEAD_DIM), F32),
            vmem((seq_size, slice_rows + 8, HEAD_DIM), F32),
            vmem((seq_size, slice_rows, HEAD_DIM), F32),
            vmem((seq_size, slice_rows, HEAD_DIM), F32),
            vmem((tokens, FEATURES), F32),
            vmem((tokens, FEATURES), F32),
            vmem((tokens, FEATURES), F32),
            vmem((2, HEADS, HEAD_DIM, HEAD_DIM), BF16),
            vmem((BLOCKS, 2, HALF, FEATURES), F32),
            vmem((BLOCKS, HALF, FEATURES), F32),
            vmem((CHUNKS, HALF, CHUNK), F32),
            vmem((CHUNKS, HALF, CHUNK), F32),
            vmem((CHUNKS, HALF, CHUNK), F32),
            vmem((CHUNKS, HALF, CHUNK), F32),
            vmem((CHUNKS, HALF, CHUNK), F32),
            vmem((CHUNKS, HALF, CHUNK), F32),
            vmem((CHUNKS, HALF, CHUNK), F32),
            vmem((HALF, WIDTH), BF16),
            dma((6,)), dma((2,)), dma((2,)), dma((CHUNKS,)), dma((CHUNKS,)), dma((BLOCKS,)), dma((BLOCKS,)),
            dma((3, CHUNKS)), dma((3, CHUNKS)), dma((CHUNKS,)),
        ],
        compiler_params=pltpu.CompilerParams(
            collective_id=0, has_side_effects=True, vmem_limit_bytes=62 * 1024 * 1024
        ),
    )(log_decay.T, key_vectors, value_vectors, queries, gate_input, out_weight)


def solution(mesh):
    placed = (
        P("seq", "head"),
        P("seq", "head"),
        P("seq", "head"),
        P("seq", "head"),
        P("seq", "head"),
        P("head", None),
    )
    return jax.shard_map(
        functools.partial(per_device, mesh.shape["seq"]),
        mesh=mesh, in_specs=placed, out_specs=P(("seq", "head"), None), check_vma=False,
    )
```

```python
import functools

import jax
import jax.numpy as jnp
from jax import lax
from jax.experimental import pallas as pl
from jax.experimental.pallas import tpu as pltpu
from jax.sharding import PartitionSpec as P

HEAD_DIM = 128
BLOCK = 256
HALF = 128
HEADS = 4
BLOCKS = 4
FEATURES = HEADS * HEAD_DIM
WIDTH = 4096
CHUNK = 512
CHUNKS = WIDTH // CHUNK
RING = CHUNKS // 2
SIDE = RING // 2
QUARTERS = CHUNKS - RING
XS = 4
F32 = jnp.float32
BF16 = jnp.bfloat16
MESH = pl.DeviceIdType.MESH
NT = (((1,), (1,)), ((), ()))
TN = (((0,), (0,)), ((), ()))


def head_columns(h):
    return slice(h * HEAD_DIM, (h + 1) * HEAD_DIM)


def kernel(
    seq_size, rate_hbm, k_hbm, v_hbm, q_hbm, g_hbm, w_hbm, out_ref,
    rate, padded, k, v, q, g, w, w_send, w_recv, w_pair,
    run_col, run_row, start, lead, state_send, state_recv, scan_send, scan_recv,
    att, since, silu, entry, hid, hid_recv, far, plus, minus, own, far_recv, direct_recv,
    sum_recv, result, quarter, w_mate, hid_mate, pair_out, pair_in, pair_own,
    load_sem, a_send, a_recv, w_ssem, w_rsem, h_ssem, h_rsem,
    y_send, y_recv, o_sem, line_sem, q_send, q_recv, x_send, x_recv, d_send, d_recv,
    m_send, m_recv, g_send, g_recv,
):
    me = lax.axis_index("seq")
    head = lax.axis_index("head")
    row = head // 2
    core = lax.rem(head, 2)
    partner = row * 2 + (1 - core)
    up = lax.rem(row + 1, 4) * 2 + core
    down = lax.rem(row + 3, 4) * 2 + core
    slice_rows = FEATURES // seq_size
    per_head = HEAD_DIM // slice_rows
    odd = lax.rem(row, 2)
    mate = (row + 1 - 2 * odd) * 2 + core
    cross = lax.rem(row + 3 + 2 * odd, 4) * 2 + core
    x = lax.rem(me, XS)
    x_up = me - x + lax.rem(x + 1, XS)
    x_down = me - x + lax.rem(x + 3, XS)

    loads = [
        pltpu.make_async_copy(src, dst, load_sem.at[i])
        for i, (src, dst) in enumerate(
            ((rate_hbm, rate), (k_hbm, k), (v_hbm, v), (q_hbm, q), (w_hbm, w), (g_hbm, g))
        )
    ]
    for load in loads[:3]:
        load.start()

    barrier = pltpu.get_barrier_semaphore()

    def greet(peer):
        pl.semaphore_signal(barrier, inc=1, device_id=(peer, head), device_id_type=MESH)

    zs = seq_size // XS
    x_line = [me - x + lax.rem(x + d, XS) for d in range(1, XS)]
    for peer in x_line:
        greet(peer)
    for d in range(1, zs):
        greet(lax.rem(me + d * XS, seq_size))
    for other in (partner, up, down):
        pl.semaphore_signal(barrier, inc=1, device_id=(me, other), device_id_type=MESH)

    low = lax.broadcasted_iota(jnp.int32, (BLOCK, BLOCK), 0)
    high = lax.broadcasted_iota(jnp.int32, (BLOCK, BLOCK), 1)
    upper = jnp.where(low <= high, 1.0, 0.0).astype(BF16)
    lower = jnp.where(low >= high, 1.0, 0.0).astype(BF16)
    loads[0].wait()
    for b in range(BLOCKS):
        padded[b, 0:HEADS, :] = rate[:, b * BLOCK:(b + 1) * BLOCK]
        padded[b, HEADS:8, :] = jnp.zeros((8 - HEADS, BLOCK), F32)
    rates = padded[...].reshape(BLOCKS * 8, BLOCK)
    run_rows = jnp.zeros((BLOCKS * 8, BLOCK), F32)
    run_cols = jnp.zeros((BLOCK, BLOCKS * 8), F32)
    for _ in range(3):
        piece = rates.astype(BF16)
        run_rows += jnp.dot(piece, upper, preferred_element_type=F32)
        run_cols += lax.dot_general(lower, piece, NT, preferred_element_type=F32)
        rates = rates - piece.astype(F32)
    run_row[...] = run_rows.reshape(BLOCKS, 8, BLOCK)
    for b in range(BLOCKS):
        run_col[b] = run_cols[:, 8 * b:8 * b + 8]
    totals = run_rows[:, BLOCK - 1:BLOCK]
    key_scale = jnp.exp(totals - run_rows)
    block_decay = jnp.broadcast_to(jnp.exp(totals), (BLOCKS * 8, HEAD_DIM))
    ahead = jnp.zeros((8, 1), F32)
    for b in range(BLOCKS):
        lead[b] = jnp.broadcast_to(jnp.exp(ahead), (8, HEAD_DIM))
        ahead = ahead + totals[8 * b:8 * b + 8]
    through = jnp.broadcast_to(jnp.exp(ahead), (8, HEAD_DIM))
    pl.semaphore_wait(barrier, XS - 1 + zs - 1 + 3)
    for peer in x_line:
        pl.semaphore_signal(line_sem, inc=1, device_id=(peer, head), device_id_type=MESH)
    loads[1].wait()
    loads[2].wait()
    for load in loads[3:]:
        load.start()
    for h in range(HEADS):
        state = jnp.zeros((HEAD_DIM, HEAD_DIM), F32)
        for b in range(BLOCKS):
            rows = slice(b * BLOCK, (b + 1) * BLOCK)
            line = slice(8 * b + h, 8 * b + h + 1)
            start[b, h] = state
            keys = (k[rows, head_columns(h)].T.astype(F32) * key_scale[line]).astype(BF16)
            added = jnp.dot(keys, v[rows, head_columns(h)], preferred_element_type=F32)
            state = block_decay[line] * state + added
        pieces = pl.ds(h * per_head, per_head)
        state_send[pieces, 0:slice_rows, :] = state.reshape(per_head, slice_rows, HEAD_DIM)
        state_send[pieces, slice_rows:slice_rows + 8, :] = jnp.broadcast_to(
            through[h:h + 1], (per_head, 8, HEAD_DIM)
        )

    pl.semaphore_wait(line_sem, XS - 1)

    def exchange(phase, src, dst, peer):
        return pltpu.make_async_remote_copy(
            src_ref=src, dst_ref=dst, send_sem=a_send.at[phase], recv_sem=a_recv.at[phase],
            device_id=(peer, head), device_id_type=MESH,
        )

    others = pl.ds(0, seq_size - 1)
    next_peer = lax.rem(me + 1, seq_size)
    message = pl.ds(0, slice_rows + 1)
    all_slices = exchange(
        0, state_send.at[others, message], state_recv.at[others, message], next_peer
    )
    all_scans = exchange(1, scan_send.at[others], scan_recv.at[others], next_peer)

    def each_peer(send):
        send(lax.rem(me + seq_size // 2, seq_size))

        def both_ways(d, carry):
            send(lax.rem(me + seq_size // 2 + d, seq_size))
            send(lax.rem(me + seq_size // 2 - d, seq_size))
            return carry

        lax.fori_loop(1, seq_size // 2, both_ways, 0)

    def send_slice(peer):
        exchange(0, state_send.at[peer, message], state_recv.at[me, message], peer).start()

    each_peer(send_slice)
    state_recv[me] = state_send[me]

    blocks = [lax.rem(row + 2, 4), lax.rem(row + 1, 4), lax.rem(row + 3, 4), row]
    order = [n // 2 + (n % 2) * SIDE for n in range(RING)]

    def columns(n):
        return slice(n * CHUNK, (n + 1) * CHUNK)

    loads[4].wait()

    def remote(src, dst, send_sem, recv_sem, device):
        return pltpu.make_async_remote_copy(
            src_ref=src, dst_ref=dst, send_sem=send_sem, recv_sem=recv_sem,
            device_id=device, device_id_type=MESH,
        )

    def paired_columns(part):
        return pl.ds(pl.multiple_of((RING + part) * CHUNK, CHUNK), CHUNK)

    deep = FEATURES // 2
    quarter_copies = []
    for i in range(2):
        quarter[i] = w[i * deep:(i + 1) * deep, paired_columns(x)].astype(F32)
        quarter_copies.append(
            remote(quarter.at[i], w_mate.at[0, x, i], q_send.at[i], q_recv.at[i], (me, mate))
        )
        quarter_copies[-1].start()
    parts = [x, lax.rem(x + 3, XS), lax.rem(x + 1, XS), lax.rem(x + 2, XS)]
    x_copies = []
    for i in range(2):
        x_copies.append([
            remote(
                w_mate.at[0, x, i], w_mate.at[0, x, i], x_send.at[side, i], x_recv.at[side, i],
                (peer, head),
            )
            for side, peer in ((0, x_up), (1, x_down))
        ])
    relay_up = remote(
        w_mate.at[0, parts[1], 0], w_mate.at[0, parts[1], 0], x_send.at[0, 2], x_recv.at[0, 2],
        (x_up, head),
    )
    relay_down = remote(
        w_mate.at[0, parts[2], 1], w_mate.at[0, parts[2], 1], x_send.at[1, 2], x_recv.at[1, 2],
        (x_down, head),
    )
    share_copies = [
        remote(w_mate.at[0, part], w_mate.at[1, part], d_send.at[j], d_recv.at[j], (me, partner))
        for j, part in enumerate(parts)
    ]

    pair_copies = {}
    for n in order + list(range(RING, CHUNKS)):
        w_send[n] = w[:, columns(n)].astype(F32)
        pair_copies[n] = pltpu.make_async_remote_copy(
            src_ref=w_send.at[n], dst_ref=w_recv.at[n],
            send_sem=w_ssem.at[n], recv_sem=w_rsem.at[n],
            device_id=(me, partner), device_id_type=MESH,
        )
        pair_copies[n].start()

    def receive_weights(n):
        pair_copies[n].wait_recv()
        w_pair[:, columns(n)] = w_recv[n].astype(BF16)

    loads[3].wait()
    loads[5].wait()
    causal = low >= high

    def inside(b):
        rows = pl.ds(pl.multiple_of(b * BLOCK, BLOCK), BLOCK)
        for h in range(HEADS):
            scores = lax.dot_general(
                q[rows, head_columns(h)], k[rows, head_columns(h)], NT,
                preferred_element_type=F32,
            )
            run = run_col[b, :, h:h + 1]
            decay = jnp.exp(jnp.where(causal, run - run_row[b, h:h + 1, :], -1e30))
            weights = (scores * decay).astype(BF16)
            att[rows, head_columns(h)] = jnp.dot(
                weights, v[rows, head_columns(h)], preferred_element_type=F32
            )
            since[rows, head_columns(h)] = jnp.broadcast_to(jnp.exp(run), (BLOCK, HEAD_DIM))
            gate = g[rows, head_columns(h)].astype(F32)
            silu[rows, head_columns(h)] = gate / (1.0 + jnp.exp(-gate))

    inside(blocks[0])
    inside(blocks[1])

    all_slices.wait_recv()

    def scan(p, state):
        scan_send[p] = state
        return state_recv[p, slice_rows:slice_rows + 1, :] * state + state_recv[p, 0:slice_rows, :]

    lax.fori_loop(0, seq_size, scan, jnp.zeros((slice_rows, HEAD_DIM), F32), unroll=4)

    def send_scan(peer):
        exchange(1, scan_send.at[peer], scan_recv.at[me], peer).start()

    each_peer(send_scan)
    scan_recv[me] = scan_send[me]

    inside(blocks[2])
    inside(blocks[3])
    for n in order:
        receive_weights(n)
    quarter_copies[0].wait_recv()
    for copy in x_copies[0]:
        copy.start()
    all_scans.wait_recv()

    hid_copies = []

    def hide(t):
        b = blocks[t]
        for h in range(HEADS):
            incoming = scan_recv[h * per_head:(h + 1) * per_head].reshape(HEAD_DIM, HEAD_DIM)
            state = start[b, h] + lead[b, h:h + 1, :] * incoming
            top = state.astype(BF16)
            entry[0, h] = top
            entry[1, h] = (state - top.astype(F32)).astype(BF16)
        for side in (1 - core, core):
            rows = pl.ds(pl.multiple_of(b * BLOCK + side * HALF, HALF), HALF)
            for h in range(HEADS):
                queries = q[rows, head_columns(h)]
                carried = jnp.dot(queries, entry[0, h], preferred_element_type=F32) + jnp.dot(
                    queries, entry[1, h], preferred_element_type=F32
                )
                attended = att[rows, head_columns(h)] + carried * since[rows, head_columns(h)]
                mean = jnp.mean(attended * attended, axis=-1, keepdims=True)
                gated = attended * lax.rsqrt(mean + 1e-6) * silu[rows, head_columns(h)]
                hid[t, side, :, head_columns(h)] = gated.astype(BF16).astype(F32)
            if side is not core:
                copy = pltpu.make_async_remote_copy(
                    src_ref=hid.at[t, 1 - core], dst_ref=hid_recv.at[t],
                    send_sem=h_ssem.at[t], recv_sem=h_rsem.at[t],
                    device_id=(me, partner), device_id_type=MESH,
                )
                copy.start()
                hid_copies.append(copy)

    def project(t, n):
        return jnp.dot(
            hid[t, core].astype(BF16), w[:, columns(n)], preferred_element_type=F32
        ) + jnp.dot(hid_recv[t].astype(BF16), w_pair[:, columns(n)], preferred_element_type=F32)

    def across(kind, n, src, dst, other):
        return pltpu.make_async_remote_copy(
            src_ref=src, dst_ref=dst, send_sem=y_send.at[kind, n], recv_sem=y_recv.at[kind, n],
            device_id=(me, other), device_id_type=MESH,
        )

    far_copies = [
        across(0, n, far.at[n], far_recv.at[n], up if n < SIDE else down) for n in range(RING)
    ]
    direct_copies = [
        across(
            1, n, minus.at[n] if n < SIDE else plus.at[n], direct_recv.at[n],
            down if n < SIDE else up,
        )
        for n in range(RING)
    ]
    sum_copies = [
        across(
            2, n, plus.at[n] if n < SIDE else minus.at[n], sum_recv.at[n],
            up if n < SIDE else down,
        )
        for n in range(RING)
    ]
    mate_turn, cross_turn = 1 + odd, 2 - odd
    mate_copies = []
    for block, t in enumerate((0, mate_turn)):
        for i, src in enumerate((hid.at[t, core], hid_recv.at[t])):
            mate_copies.append(
                remote(
                    src, hid_mate.at[block, i], m_send.at[block, i], m_recv.at[block, i], (me, mate)
                )
            )
    cross_copies = [
        remote(pair_out.at[j], pair_in.at[j], g_send.at[j], g_recv.at[j], (me, cross))
        for j in range(QUARTERS)
    ]

    def paired(block, t, part):
        products = (
            (hid[t, core], w[:, paired_columns(part)]),
            (hid_recv[t], w_recv[RING + part].astype(BF16)),
            (hid_mate[block, 0], w_mate[0, part].reshape(FEATURES, CHUNK).astype(BF16)),
            (hid_mate[block, 1], w_mate[1, part].reshape(FEATURES, CHUNK).astype(BF16)),
        )
        total = jnp.zeros((HALF, CHUNK), F32)
        for left, right in products:
            total += jnp.dot(left.astype(BF16), right, preferred_element_type=F32)
        return total

    def cross_out(j):
        share_copies[j].wait_recv()
        pair_out[j] = paired(0, cross_turn, parts[j])
        cross_copies[j].start()

    hide(0)
    hid_copies[0].wait_recv()
    for copy in mate_copies[:2]:
        copy.start()
    for n in order:
        far[n] = project(0, n)
        far_copies[n].start()
    quarter_copies[1].wait_recv()
    for copy in x_copies[1]:
        copy.start()
    share_copies[0].start()
    hide(1)
    hide(2)
    hid_copies[1].wait_recv()
    for n in range(SIDE, RING):
        plus[n] = project(1, n)
        direct_copies[n].start()
    hid_copies[2].wait_recv()
    for n in range(SIDE):
        minus[n] = project(2, n)
        direct_copies[n].start()
    for copy in mate_copies[2:]:
        copy.start()
    x_copies[0][0].wait_recv()
    relay_up.start()
    for n in range(SIDE):
        plus[n] = project(1, n)
        minus[SIDE + n] = project(2, SIDE + n)
    hide(3)
    hid_copies[3].wait_recv()
    for n in order:
        own[n] = project(3, n)
    for n in range(RING, CHUNKS):
        pair_copies[n].wait_recv()
    x_copies[0][1].wait_recv()
    x_copies[1][1].wait_recv()
    relay_down.start()
    share_copies[2].start()
    x_copies[1][0].wait_recv()
    share_copies[1].start()
    for copy in mate_copies[:2]:
        copy.wait_recv()
    cross_out(0)
    for n in range(SIDE):
        far_copies[n].wait_recv()
        plus[n] += far_recv[n]
        sum_copies[n].start()
        far_copies[SIDE + n].wait_recv()
        minus[SIDE + n] += far_recv[SIDE + n]
        sum_copies[SIDE + n].start()
    cross_out(1)
    cross_out(2)
    relay_up.wait_recv()
    relay_down.wait_recv()
    share_copies[3].start()
    cross_out(3)
    for n in order:
        direct_copies[n].wait_recv()
        own[n] += direct_recv[n]
    for copy in mate_copies[2:]:
        copy.wait_recv()
    for j in range(QUARTERS):
        pair_own[j] = paired(1, 3, parts[j])
    out_copies = []

    def put(i, where, value):
        result[:, where] = value.astype(BF16)
        out_copies.append(
            pltpu.make_async_copy(result.at[:, where], out_ref.at[:, where], o_sem.at[i])
        )
        out_copies[-1].start()

    for j, n in enumerate(order):
        cross_copies[j].wait_recv()
        put(RING + j, paired_columns(parts[j]), pair_own[j] + pair_in[j])
        sum_copies[n].wait_recv()
        put(n, columns(n), own[n] + sum_recv[n])

    all_slices.wait_send()
    all_scans.wait_send()
    for copy in list(pair_copies.values()) + hid_copies + far_copies + direct_copies + sum_copies:
        copy.wait_send()
    for copy in quarter_copies + x_copies[0] + x_copies[1] + [relay_up, relay_down]:
        copy.wait_send()
    for copy in share_copies + mate_copies + cross_copies:
        copy.wait_send()
    for copy in out_copies:
        copy.wait()


def per_device(seq_size, queries, key_vectors, value_vectors, gate_input, log_decay, out_weight):
    tokens = BLOCKS * BLOCK
    slice_rows = FEATURES // seq_size
    whole = pl.BlockSpec(memory_space=pl.ANY)
    dma = pltpu.SemaphoreType.DMA
    vmem = pltpu.VMEM
    return pl.pallas_call(
        functools.partial(kernel, seq_size),
        out_shape=jax.ShapeDtypeStruct((HALF, WIDTH), BF16),
        in_specs=[whole] * 6,
        out_specs=whole,
        scratch_shapes=[
            vmem((HEADS, tokens), F32),
            vmem((BLOCKS, 8, BLOCK), F32),
            vmem((tokens, FEATURES), BF16),
            vmem((tokens, FEATURES), BF16),
            vmem((tokens, FEATURES), BF16),
            vmem((tokens, FEATURES), BF16),
            vmem((FEATURES, WIDTH), BF16),
            vmem((CHUNKS, FEATURES, CHUNK), F32),
            vmem((CHUNKS, FEATURES, CHUNK), F32),
            vmem((FEATURES, RING * CHUNK), BF16),
            vmem((BLOCKS, BLOCK, 8), F32),
            vmem((BLOCKS, 8, BLOCK), F32),
            vmem((BLOCKS, HEADS, HEAD_DIM, HEAD_DIM), F32),
            vmem((BLOCKS, 8, HEAD_DIM), F32),
            vmem((seq_size, slice_rows + 8, HEAD_DIM), F32),
            vmem((seq_size, slice_rows + 8, HEAD_DIM), F32),
            vmem((seq_size, slice_rows, HEAD_DIM), F32),
            vmem((seq_size, slice_rows, HEAD_DIM), F32),
            vmem((tokens, FEATURES), F32),
            vmem((tokens, FEATURES), F32),
            vmem((tokens, FEATURES), F32),
            vmem((2, HEADS, HEAD_DIM, HEAD_DIM), BF16),
            vmem((BLOCKS, 2, HALF, FEATURES), F32),
            vmem((BLOCKS, HALF, FEATURES), F32),
            vmem((RING, HALF, CHUNK), F32),
            vmem((RING, HALF, CHUNK), F32),
            vmem((RING, HALF, CHUNK), F32),
            vmem((RING, HALF, CHUNK), F32),
            vmem((RING, HALF, CHUNK), F32),
            vmem((RING, HALF, CHUNK), F32),
            vmem((RING, HALF, CHUNK), F32),
            vmem((HALF, WIDTH), BF16),
            vmem((2, FEATURES // 2, CHUNK), F32),
            vmem((2, QUARTERS, 2, FEATURES // 2, CHUNK), F32),
            vmem((2, 2, HALF, FEATURES), F32),
            vmem((QUARTERS, HALF, CHUNK), F32),
            vmem((QUARTERS, HALF, CHUNK), F32),
            vmem((QUARTERS, HALF, CHUNK), F32),
            dma((6,)), dma((2,)), dma((2,)), dma((CHUNKS,)), dma((CHUNKS,)), dma((BLOCKS,)), dma((BLOCKS,)),
            dma((3, RING)), dma((3, RING)), dma((CHUNKS,)),
            pltpu.SemaphoreType.REGULAR, dma((2,)), dma((2,)), dma((2, 3)), dma((2, 3)),
            dma((QUARTERS,)), dma((QUARTERS,)), dma((2, 2)), dma((2, 2)),
            dma((QUARTERS,)), dma((QUARTERS,)),
        ],
        compiler_params=pltpu.CompilerParams(
            collective_id=0, has_side_effects=True, vmem_limit_bytes=67043328
        ),
    )(log_decay.T, key_vectors, value_vectors, queries, gate_input, out_weight)


def solution(mesh):
    placed = (
        P("seq", "head"),
        P("seq", "head"),
        P("seq", "head"),
        P("seq", "head"),
        P("seq", "head"),
        P("head", None),
    )
    return jax.shard_map(
        functools.partial(per_device, mesh.shape["seq"]),
        mesh=mesh, in_specs=placed, out_specs=P(("seq", "head"), None), check_vma=False,
    )
```

```python
import functools

import jax
import jax.numpy as jnp
from jax import lax
from jax.experimental import pallas as pl
from jax.experimental.pallas import tpu as pltpu
from jax.sharding import PartitionSpec as P

HEAD_DIM = 128
BLOCK = 256
HALF = 128
HEADS = 4
BLOCKS = 4
FEATURES = HEADS * HEAD_DIM
WIDTH = 4096
CHUNK = 512
CHUNKS = WIDTH // CHUNK
RING = CHUNKS // 2
SIDE = RING // 2
QUARTERS = CHUNKS - RING
XS = 4
F32 = jnp.float32
BF16 = jnp.bfloat16
MESH = pl.DeviceIdType.MESH
NT = (((1,), (1,)), ((), ()))
TN = (((0,), (0,)), ((), ()))


def head_columns(h):
    return slice(h * HEAD_DIM, (h + 1) * HEAD_DIM)


def kernel(
    seq_size, rate_hbm, k_hbm, v_hbm, q_hbm, g_hbm, w_hbm, out_ref,
    rate, padded, k, v, q, g, w, w_send, w_recv, w_pair,
    run_col, run_row, start, lead, state_send, state_recv, scan_send, scan_recv,
    att, since, silu, entry, hid, hid_recv, far, plus, minus, own, far_recv, direct_recv,
    sum_recv, quarter, w_mate, hid_mate, pair_out, pair_in, pair_own,
    load_sem, a_send, a_recv, w_ssem, w_rsem, h_ssem, h_rsem,
    y_send, y_recv, line_sem, q_send, q_recv, x_send, x_recv, d_send, d_recv,
    m_send, m_recv, g_send, g_recv,
):
    me = lax.axis_index("seq")
    head = lax.axis_index("head")
    row = head // 2
    core = lax.rem(head, 2)
    partner = row * 2 + (1 - core)
    up = lax.rem(row + 1, 4) * 2 + core
    down = lax.rem(row + 3, 4) * 2 + core
    slice_rows = FEATURES // seq_size
    per_head = HEAD_DIM // slice_rows
    odd = lax.rem(row, 2)
    mate = (row + 1 - 2 * odd) * 2 + core
    cross = lax.rem(row + 3 + 2 * odd, 4) * 2 + core
    x = lax.rem(me, XS)
    x_up = me - x + lax.rem(x + 1, XS)
    x_down = me - x + lax.rem(x + 3, XS)
    half = lax.rem(me // XS, 2)
    z_pair = me + XS * (1 - 2 * half)
    halves = (half, 1 - half)

    loads = [
        pltpu.make_async_copy(src, dst, load_sem.at[i])
        for i, (src, dst) in enumerate(
            ((rate_hbm, rate), (k_hbm, k), (v_hbm, v), (q_hbm, q), (w_hbm, w), (g_hbm, g))
        )
    ]
    for load in loads[:3]:
        load.start()

    barrier = pltpu.get_barrier_semaphore()

    def greet(peer):
        pl.semaphore_signal(barrier, inc=1, device_id=(peer, head), device_id_type=MESH)

    zs = seq_size // XS
    x_line = [me - x + lax.rem(x + d, XS) for d in range(1, XS)]
    for peer in x_line:
        greet(peer)
    for d in range(1, zs):
        greet(lax.rem(me + d * XS, seq_size))
    for other in (partner, up, down):
        pl.semaphore_signal(barrier, inc=1, device_id=(me, other), device_id_type=MESH)

    low = lax.broadcasted_iota(jnp.int32, (BLOCK, BLOCK), 0)
    high = lax.broadcasted_iota(jnp.int32, (BLOCK, BLOCK), 1)
    upper = jnp.where(low <= high, 1.0, 0.0).astype(BF16)
    lower = jnp.where(low >= high, 1.0, 0.0).astype(BF16)
    loads[0].wait()
    for b in range(BLOCKS):
        padded[b, 0:HEADS, :] = rate[:, b * BLOCK:(b + 1) * BLOCK]
        padded[b, HEADS:8, :] = jnp.zeros((8 - HEADS, BLOCK), F32)
    rates = padded[...].reshape(BLOCKS * 8, BLOCK)
    run_rows = jnp.zeros((BLOCKS * 8, BLOCK), F32)
    run_cols = jnp.zeros((BLOCK, BLOCKS * 8), F32)
    for _ in range(3):
        piece = rates.astype(BF16)
        run_rows += jnp.dot(piece, upper, preferred_element_type=F32)
        run_cols += lax.dot_general(lower, piece, NT, preferred_element_type=F32)
        rates = rates - piece.astype(F32)
    run_row[...] = run_rows.reshape(BLOCKS, 8, BLOCK)
    for b in range(BLOCKS):
        run_col[b] = run_cols[:, 8 * b:8 * b + 8]
    totals = run_rows[:, BLOCK - 1:BLOCK]
    key_scale = jnp.exp(totals - run_rows)
    block_decay = jnp.broadcast_to(jnp.exp(totals), (BLOCKS * 8, HEAD_DIM))
    ahead = jnp.zeros((8, 1), F32)
    for b in range(BLOCKS):
        lead[b] = jnp.broadcast_to(jnp.exp(ahead), (8, HEAD_DIM))
        ahead = ahead + totals[8 * b:8 * b + 8]
    through = jnp.broadcast_to(jnp.exp(ahead), (8, HEAD_DIM))
    pl.semaphore_wait(barrier, XS - 1 + zs - 1 + 3)
    for peer in x_line:
        pl.semaphore_signal(line_sem, inc=1, device_id=(peer, head), device_id_type=MESH)
    loads[1].wait()
    loads[2].wait()
    for load in loads[3:]:
        load.start()
    for h in range(HEADS):
        state = jnp.zeros((HEAD_DIM, HEAD_DIM), F32)
        for b in range(BLOCKS):
            rows = slice(b * BLOCK, (b + 1) * BLOCK)
            line = slice(8 * b + h, 8 * b + h + 1)
            start[b, h] = state
            keys = (k[rows, head_columns(h)].T.astype(F32) * key_scale[line]).astype(BF16)
            added = jnp.dot(keys, v[rows, head_columns(h)], preferred_element_type=F32)
            state = block_decay[line] * state + added
        pieces = pl.ds(h * per_head, per_head)
        state_send[pieces, 0:slice_rows, :] = state.reshape(per_head, slice_rows, HEAD_DIM)
        state_send[pieces, slice_rows:slice_rows + 8, :] = jnp.broadcast_to(
            through[h:h + 1], (per_head, 8, HEAD_DIM)
        )

    pl.semaphore_wait(line_sem, XS - 1)

    def exchange(phase, src, dst, peer):
        return pltpu.make_async_remote_copy(
            src_ref=src, dst_ref=dst, send_sem=a_send.at[phase], recv_sem=a_recv.at[phase],
            device_id=(peer, head), device_id_type=MESH,
        )

    others = pl.ds(0, seq_size - 1)
    next_peer = lax.rem(me + 1, seq_size)
    message = pl.ds(0, slice_rows + 1)
    all_slices = exchange(
        0, state_send.at[others, message], state_recv.at[others, message], next_peer
    )
    all_scans = exchange(1, scan_send.at[others], scan_recv.at[others], next_peer)

    def each_peer(send):
        send(lax.rem(me + seq_size // 2, seq_size))

        def both_ways(d, carry):
            send(lax.rem(me + seq_size // 2 + d, seq_size))
            send(lax.rem(me + seq_size // 2 - d, seq_size))
            return carry

        lax.fori_loop(1, seq_size // 2, both_ways, 0)

    def send_slice(peer):
        exchange(0, state_send.at[peer, message], state_recv.at[me, message], peer).start()

    each_peer(send_slice)
    state_recv[me] = state_send[me]

    blocks = [lax.rem(row + 2, 4), lax.rem(row + 1, 4), lax.rem(row + 3, 4), row]
    order = [n // 2 + (n % 2) * SIDE for n in range(RING)]

    def columns(n):
        return slice(n * CHUNK, (n + 1) * CHUNK)

    loads[4].wait()

    def remote(src, dst, send_sem, recv_sem, device):
        return pltpu.make_async_remote_copy(
            src_ref=src, dst_ref=dst, send_sem=send_sem, recv_sem=recv_sem,
            device_id=device, device_id_type=MESH,
        )

    def paired_columns(part):
        return pl.ds(pl.multiple_of((RING + part) * CHUNK, CHUNK), CHUNK)

    deep = FEATURES // 2
    rows = pl.ds(pl.multiple_of(half * deep, deep), deep)
    quarter[...] = w[rows, paired_columns(x)].astype(F32)
    quarter_copies = [
        remote(quarter, w_mate.at[0, x, half], q_send.at[0], q_recv.at[0], (me, mate)),
        remote(
            w_mate.at[0, x, half], w_mate.at[0, x, half], q_send.at[1], q_recv.at[1],
            (z_pair, head),
        ),
    ]
    quarter_copies[0].start()
    parts = [x, lax.rem(x + 3, XS), lax.rem(x + 1, XS), lax.rem(x + 2, XS)]
    x_copies = []
    for i in range(2):
        x_copies.append([
            remote(
                w_mate.at[0, x, halves[i]], w_mate.at[0, x, halves[i]], x_send.at[side, i],
                x_recv.at[side, i],
                (peer, head),
            )
            for side, peer in ((0, x_up), (1, x_down))
        ])
    relay_up = remote(
        w_mate.at[0, parts[1], half], w_mate.at[0, parts[1], half], x_send.at[0, 2], x_recv.at[0, 2],
        (x_up, head),
    )
    relay_down = remote(
        w_mate.at[0, parts[2], 1 - half], w_mate.at[0, parts[2], 1 - half], x_send.at[1, 2], x_recv.at[1, 2],
        (x_down, head),
    )
    share_copies = [
        remote(w_mate.at[0, part], w_mate.at[1, part], d_send.at[j], d_recv.at[j], (me, partner))
        for j, part in enumerate(parts)
    ]

    pair_copies = {}
    for n in order + list(range(RING, CHUNKS)):
        w_send[n] = w[:, columns(n)].astype(F32)
        pair_copies[n] = pltpu.make_async_remote_copy(
            src_ref=w_send.at[n], dst_ref=w_recv.at[n],
            send_sem=w_ssem.at[n], recv_sem=w_rsem.at[n],
            device_id=(me, partner), device_id_type=MESH,
        )
        pair_copies[n].start()

    def receive_weights(n):
        pair_copies[n].wait_recv()
        w_pair[:, columns(n)] = w_recv[n].astype(BF16)

    loads[3].wait()
    loads[5].wait()
    causal = low >= high

    def inside(b):
        rows = pl.ds(pl.multiple_of(b * BLOCK, BLOCK), BLOCK)
        for h in range(HEADS):
            scores = lax.dot_general(
                q[rows, head_columns(h)], k[rows, head_columns(h)], NT,
                preferred_element_type=F32,
            )
            run = run_col[b, :, h:h + 1]
            decay = jnp.exp(jnp.where(causal, run - run_row[b, h:h + 1, :], -1e30))
            weights = (scores * decay).astype(BF16)
            att[rows, head_columns(h)] = jnp.dot(
                weights, v[rows, head_columns(h)], preferred_element_type=F32
            )
            since[rows, head_columns(h)] = jnp.broadcast_to(jnp.exp(run), (BLOCK, HEAD_DIM))
            gate = g[rows, head_columns(h)].astype(F32)
            silu[rows, head_columns(h)] = gate / (1.0 + jnp.exp(-gate))

    inside(blocks[0])
    inside(blocks[1])

    all_slices.wait_recv()

    def scan(p, state):
        scan_send[p] = state
        return state_recv[p, slice_rows:slice_rows + 1, :] * state + state_recv[p, 0:slice_rows, :]

    lax.fori_loop(0, seq_size, scan, jnp.zeros((slice_rows, HEAD_DIM), F32), unroll=4)

    def send_scan(peer):
        exchange(1, scan_send.at[peer], scan_recv.at[me], peer).start()

    each_peer(send_scan)
    scan_recv[me] = scan_send[me]

    inside(blocks[2])
    inside(blocks[3])
    for n in order:
        receive_weights(n)
    quarter_copies[0].wait_recv()
    for copy in x_copies[0]:
        copy.start()
    all_scans.wait_recv()
    quarter_copies[1].start()

    hid_copies = []

    def hide(t):
        b = blocks[t]
        for h in range(HEADS):
            incoming = scan_recv[h * per_head:(h + 1) * per_head].reshape(HEAD_DIM, HEAD_DIM)
            state = start[b, h] + lead[b, h:h + 1, :] * incoming
            top = state.astype(BF16)
            entry[0, h] = top
            entry[1, h] = (state - top.astype(F32)).astype(BF16)
        for side in (1 - core, core):
            rows = pl.ds(pl.multiple_of(b * BLOCK + side * HALF, HALF), HALF)
            for h in range(HEADS):
                queries = q[rows, head_columns(h)]
                carried = jnp.dot(queries, entry[0, h], preferred_element_type=F32) + jnp.dot(
                    queries, entry[1, h], preferred_element_type=F32
                )
                attended = att[rows, head_columns(h)] + carried * since[rows, head_columns(h)]
                mean = jnp.mean(attended * attended, axis=-1, keepdims=True)
                gated = attended * lax.rsqrt(mean + 1e-6) * silu[rows, head_columns(h)]
                hid[t, side, :, head_columns(h)] = gated.astype(BF16).astype(F32)
            if side is not core:
                copy = pltpu.make_async_remote_copy(
                    src_ref=hid.at[t, 1 - core], dst_ref=hid_recv.at[t],
                    send_sem=h_ssem.at[t], recv_sem=h_rsem.at[t],
                    device_id=(me, partner), device_id_type=MESH,
                )
                copy.start()
                hid_copies.append(copy)

    def project(t, n):
        return jnp.dot(
            hid[t, core].astype(BF16), w[:, columns(n)], preferred_element_type=F32
        ) + jnp.dot(hid_recv[t].astype(BF16), w_pair[:, columns(n)], preferred_element_type=F32)

    def across(kind, n, src, dst, other):
        return pltpu.make_async_remote_copy(
            src_ref=src, dst_ref=dst, send_sem=y_send.at[kind, n], recv_sem=y_recv.at[kind, n],
            device_id=(me, other), device_id_type=MESH,
        )

    far_copies = [
        across(0, n, far.at[n], far_recv.at[n], up if n < SIDE else down) for n in range(RING)
    ]
    direct_copies = [
        across(
            1, n, minus.at[n] if n < SIDE else plus.at[n], direct_recv.at[n],
            down if n < SIDE else up,
        )
        for n in range(RING)
    ]
    sum_copies = [
        across(
            2, n, plus.at[n] if n < SIDE else minus.at[n], sum_recv.at[n],
            up if n < SIDE else down,
        )
        for n in range(RING)
    ]
    mate_turn, cross_turn = 1 + odd, 2 - odd
    mate_copies = []
    for block, t in enumerate((0, mate_turn)):
        for i, src in enumerate((hid.at[t, core], hid_recv.at[t])):
            mate_copies.append(
                remote(
                    src, hid_mate.at[block, i], m_send.at[block, i], m_recv.at[block, i], (me, mate)
                )
            )
    cross_copies = [
        remote(pair_out.at[j], pair_in.at[j], g_send.at[j], g_recv.at[j], (me, cross))
        for j in range(QUARTERS)
    ]

    def paired(block, t, part):
        products = (
            (hid[t, core], w[:, paired_columns(part)]),
            (hid_recv[t], w_recv[RING + part].astype(BF16)),
            (hid_mate[block, 0], w_mate[0, part].reshape(FEATURES, CHUNK).astype(BF16)),
            (hid_mate[block, 1], w_mate[1, part].reshape(FEATURES, CHUNK).astype(BF16)),
        )
        total = jnp.zeros((HALF, CHUNK), F32)
        for left, right in products:
            total += jnp.dot(left.astype(BF16), right, preferred_element_type=F32)
        return total

    def cross_out(j):
        share_copies[j].wait_recv()
        pair_out[j] = paired(0, cross_turn, parts[j])
        cross_copies[j].start()

    hide(0)
    hid_copies[0].wait_recv()
    for copy in mate_copies[:2]:
        copy.start()
    for n in order:
        far[n] = project(0, n)
        far_copies[n].start()
    quarter_copies[1].wait_recv()
    for copy in x_copies[1]:
        copy.start()
    share_copies[0].start()
    hide(1)
    hide(2)
    hid_copies[1].wait_recv()
    for n in range(SIDE, RING):
        plus[n] = project(1, n)
        direct_copies[n].start()
    hid_copies[2].wait_recv()
    for n in range(SIDE):
        minus[n] = project(2, n)
        direct_copies[n].start()
    for copy in mate_copies[2:]:
        copy.start()
    x_copies[0][0].wait_recv()
    relay_up.start()
    for n in range(SIDE):
        plus[n] = project(1, n)
        minus[SIDE + n] = project(2, SIDE + n)
    hide(3)
    hid_copies[3].wait_recv()
    for n in order:
        own[n] = project(3, n)
    for n in range(RING, CHUNKS):
        pair_copies[n].wait_recv()
    x_copies[0][1].wait_recv()
    x_copies[1][1].wait_recv()
    relay_down.start()
    share_copies[2].start()
    x_copies[1][0].wait_recv()
    share_copies[1].start()
    for copy in mate_copies[:2]:
        copy.wait_recv()
    cross_out(0)
    for n in range(SIDE):
        far_copies[n].wait_recv()
        plus[n] += far_recv[n]
        sum_copies[n].start()
        far_copies[SIDE + n].wait_recv()
        minus[SIDE + n] += far_recv[SIDE + n]
        sum_copies[SIDE + n].start()
    cross_out(1)
    cross_out(2)
    relay_up.wait_recv()
    relay_down.wait_recv()
    share_copies[3].start()
    cross_out(3)
    for n in order:
        direct_copies[n].wait_recv()
        own[n] += direct_recv[n]
    for copy in mate_copies[2:]:
        copy.wait_recv()
    for j in range(QUARTERS):
        pair_own[j] = paired(1, 3, parts[j])

    for j, n in enumerate(order):
        cross_copies[j].wait_recv()
        out_ref[:, paired_columns(parts[j])] = (pair_own[j] + pair_in[j]).astype(BF16)
        sum_copies[n].wait_recv()
        out_ref[:, columns(n)] = (own[n] + sum_recv[n]).astype(BF16)

    all_slices.wait_send()
    all_scans.wait_send()
    for copy in list(pair_copies.values()) + hid_copies + far_copies + direct_copies + sum_copies:
        copy.wait_send()
    for copy in quarter_copies + x_copies[0] + x_copies[1] + [relay_up, relay_down]:
        copy.wait_send()
    for copy in share_copies + mate_copies + cross_copies:
        copy.wait_send()


def per_device(seq_size, queries, key_vectors, value_vectors, gate_input, log_decay, out_weight):
    tokens = BLOCKS * BLOCK
    slice_rows = FEATURES // seq_size
    whole = pl.BlockSpec(memory_space=pl.ANY)
    dma = pltpu.SemaphoreType.DMA
    vmem = pltpu.VMEM
    return pl.pallas_call(
        functools.partial(kernel, seq_size),
        out_shape=pltpu.VMEM((HALF, WIDTH), BF16),
        in_specs=[whole] * 6,
        out_specs=pl.BlockSpec(memory_space=pltpu.VMEM),
        scratch_shapes=[
            vmem((HEADS, tokens), F32),
            vmem((BLOCKS, 8, BLOCK), F32),
            vmem((tokens, FEATURES), BF16),
            vmem((tokens, FEATURES), BF16),
            vmem((tokens, FEATURES), BF16),
            vmem((tokens, FEATURES), BF16),
            vmem((FEATURES, WIDTH), BF16),
            vmem((CHUNKS, FEATURES, CHUNK), F32),
            vmem((CHUNKS, FEATURES, CHUNK), F32),
            vmem((FEATURES, RING * CHUNK), BF16),
            vmem((BLOCKS, BLOCK, 8), F32),
            vmem((BLOCKS, 8, BLOCK), F32),
            vmem((BLOCKS, HEADS, HEAD_DIM, HEAD_DIM), F32),
            vmem((BLOCKS, 8, HEAD_DIM), F32),
            vmem((seq_size, slice_rows + 8, HEAD_DIM), F32),
            vmem((seq_size, slice_rows + 8, HEAD_DIM), F32),
            vmem((seq_size, slice_rows, HEAD_DIM), F32),
            vmem((seq_size, slice_rows, HEAD_DIM), F32),
            vmem((tokens, FEATURES), F32),
            vmem((tokens, FEATURES), F32),
            vmem((tokens, FEATURES), F32),
            vmem((2, HEADS, HEAD_DIM, HEAD_DIM), BF16),
            vmem((BLOCKS, 2, HALF, FEATURES), F32),
            vmem((BLOCKS, HALF, FEATURES), F32),
            vmem((RING, HALF, CHUNK), F32),
            vmem((RING, HALF, CHUNK), F32),
            vmem((RING, HALF, CHUNK), F32),
            vmem((RING, HALF, CHUNK), F32),
            vmem((RING, HALF, CHUNK), F32),
            vmem((RING, HALF, CHUNK), F32),
            vmem((RING, HALF, CHUNK), F32),
            vmem((FEATURES // 2, CHUNK), F32),
            vmem((2, QUARTERS, 2, FEATURES // 2, CHUNK), F32),
            vmem((2, 2, HALF, FEATURES), F32),
            vmem((QUARTERS, HALF, CHUNK), F32),
            vmem((QUARTERS, HALF, CHUNK), F32),
            vmem((QUARTERS, HALF, CHUNK), F32),
            dma((6,)), dma((2,)), dma((2,)), dma((CHUNKS,)), dma((CHUNKS,)), dma((BLOCKS,)), dma((BLOCKS,)),
            dma((3, RING)), dma((3, RING)),
            pltpu.SemaphoreType.REGULAR, dma((2,)), dma((2,)), dma((2, 3)), dma((2, 3)),
            dma((QUARTERS,)), dma((QUARTERS,)), dma((2, 2)), dma((2, 2)),
            dma((QUARTERS,)), dma((QUARTERS,)),
        ],
        compiler_params=pltpu.CompilerParams(
            collective_id=0, has_side_effects=True, vmem_limit_bytes=62 * 1024 * 1024
        ),
    )(log_decay.T, key_vectors, value_vectors, queries, gate_input, out_weight)


def solution(mesh):
    placed = (
        P("seq", "head"),
        P("seq", "head"),
        P("seq", "head"),
        P("seq", "head"),
        P("seq", "head"),
        P("head", None),
    )
    return jax.shard_map(
        functools.partial(per_device, mesh.shape["seq"]),
        mesh=mesh, in_specs=placed, out_specs=P(("seq", "head"), None), check_vma=False,
    )
```

```python
import functools

import jax
import jax.numpy as jnp
from jax import lax
from jax.experimental import pallas as pl
from jax.experimental.pallas import tpu as pltpu
from jax.sharding import PartitionSpec as P

HEAD_DIM = 128
BLOCK = 256
HALF = 128
HEADS = 4
BLOCKS = 4
FEATURES = HEADS * HEAD_DIM
WIDTH = 4096
RING = 4
SIDE = RING // 2
CHUNK = 384
QUARTERS = 4
PAIRED = (WIDTH - RING * CHUNK) // QUARTERS
XS = 4
F32 = jnp.float32
BF16 = jnp.bfloat16
MESH = pl.DeviceIdType.MESH
NT = (((1,), (1,)), ((), ()))
TN = (((0,), (0,)), ((), ()))


def head_columns(h):
    return slice(h * HEAD_DIM, (h + 1) * HEAD_DIM)


def kernel(
    seq_size, rate_hbm, k_hbm, v_hbm, q_hbm, g_hbm, w_hbm, out_ref,
    rate, padded, k, v, q, g, w, w_send, w_recv, p_send, p_recv, w_pair,
    run_col, run_row, start, lead, state_send, state_recv, scan_send, scan_recv,
    att, since, silu, entry, hid, hid_recv, far, plus, minus, own, far_recv, direct_recv,
    sum_recv, quarter, w_mate, hid_mate, pair_out, pair_in, pair_own,
    load_sem, a_send, a_recv, w_ssem, w_rsem, h_ssem, h_rsem,
    y_send, y_recv, line_sem, q_send, q_recv, x_send, x_recv, d_send, d_recv,
    m_send, m_recv, g_send, g_recv,
):
    me = lax.axis_index("seq")
    head = lax.axis_index("head")
    row = head // 2
    core = lax.rem(head, 2)
    partner = row * 2 + (1 - core)
    up = lax.rem(row + 1, 4) * 2 + core
    down = lax.rem(row + 3, 4) * 2 + core
    slice_rows = FEATURES // seq_size
    per_head = HEAD_DIM // slice_rows
    odd = lax.rem(row, 2)
    mate = (row + 1 - 2 * odd) * 2 + core
    cross = lax.rem(row + 3 + 2 * odd, 4) * 2 + core
    x = lax.rem(me, XS)
    x_up = me - x + lax.rem(x + 1, XS)
    x_down = me - x + lax.rem(x + 3, XS)
    half = lax.rem(me // XS, 2)
    z_pair = me + XS * (1 - 2 * half)
    halves = (half, 1 - half)

    loads = [
        pltpu.make_async_copy(src, dst, load_sem.at[i])
        for i, (src, dst) in enumerate(
            ((rate_hbm, rate), (k_hbm, k), (v_hbm, v), (q_hbm, q), (w_hbm, w), (g_hbm, g))
        )
    ]
    for load in loads[:3]:
        load.start()

    barrier = pltpu.get_barrier_semaphore()

    def greet(peer):
        pl.semaphore_signal(barrier, inc=1, device_id=(peer, head), device_id_type=MESH)

    zs = seq_size // XS
    x_line = [me - x + lax.rem(x + d, XS) for d in range(1, XS)]
    for peer in x_line:
        greet(peer)
    for d in range(1, zs):
        greet(lax.rem(me + d * XS, seq_size))
    for other in (partner, up, down):
        pl.semaphore_signal(barrier, inc=1, device_id=(me, other), device_id_type=MESH)

    low = lax.broadcasted_iota(jnp.int32, (BLOCK, BLOCK), 0)
    high = lax.broadcasted_iota(jnp.int32, (BLOCK, BLOCK), 1)
    upper = jnp.where(low <= high, 1.0, 0.0).astype(BF16)
    lower = jnp.where(low >= high, 1.0, 0.0).astype(BF16)
    loads[0].wait()
    for b in range(BLOCKS):
        padded[b, 0:HEADS, :] = rate[:, b * BLOCK:(b + 1) * BLOCK]
        padded[b, HEADS:8, :] = jnp.zeros((8 - HEADS, BLOCK), F32)
    rates = padded[...].reshape(BLOCKS * 8, BLOCK)
    run_rows = jnp.zeros((BLOCKS * 8, BLOCK), F32)
    run_cols = jnp.zeros((BLOCK, BLOCKS * 8), F32)
    for _ in range(3):
        piece = rates.astype(BF16)
        run_rows += jnp.dot(piece, upper, preferred_element_type=F32)
        run_cols += lax.dot_general(lower, piece, NT, preferred_element_type=F32)
        rates = rates - piece.astype(F32)
    run_row[...] = run_rows.reshape(BLOCKS, 8, BLOCK)
    for b in range(BLOCKS):
        run_col[b] = run_cols[:, 8 * b:8 * b + 8]
    totals = run_rows[:, BLOCK - 1:BLOCK]
    key_scale = jnp.exp(totals - run_rows)
    block_decay = jnp.broadcast_to(jnp.exp(totals), (BLOCKS * 8, HEAD_DIM))
    ahead = jnp.zeros((8, 1), F32)
    for b in range(BLOCKS):
        lead[b] = jnp.broadcast_to(jnp.exp(ahead), (8, HEAD_DIM))
        ahead = ahead + totals[8 * b:8 * b + 8]
    through = jnp.broadcast_to(jnp.exp(ahead), (8, HEAD_DIM))
    pl.semaphore_wait(barrier, XS - 1 + zs - 1 + 3)
    for peer in x_line:
        pl.semaphore_signal(line_sem, inc=1, device_id=(peer, head), device_id_type=MESH)
    loads[1].wait()
    loads[2].wait()
    for load in loads[3:]:
        load.start()
    for h in range(HEADS):
        state = jnp.zeros((HEAD_DIM, HEAD_DIM), F32)
        for b in range(BLOCKS):
            rows = slice(b * BLOCK, (b + 1) * BLOCK)
            line = slice(8 * b + h, 8 * b + h + 1)
            start[b, h] = state
            keys = (k[rows, head_columns(h)].T.astype(F32) * key_scale[line]).astype(BF16)
            added = jnp.dot(keys, v[rows, head_columns(h)], preferred_element_type=F32)
            state = block_decay[line] * state + added
        pieces = pl.ds(h * per_head, per_head)
        state_send[pieces, 0:slice_rows, :] = state.reshape(per_head, slice_rows, HEAD_DIM)
        state_send[pieces, slice_rows:slice_rows + 8, :] = jnp.broadcast_to(
            through[h:h + 1], (per_head, 8, HEAD_DIM)
        )

    pl.semaphore_wait(line_sem, XS - 1)

    def exchange(phase, src, dst, peer):
        return pltpu.make_async_remote_copy(
            src_ref=src, dst_ref=dst, send_sem=a_send.at[phase], recv_sem=a_recv.at[phase],
            device_id=(peer, head), device_id_type=MESH,
        )

    others = pl.ds(0, seq_size - 1)
    next_peer = lax.rem(me + 1, seq_size)
    message = pl.ds(0, slice_rows + 1)
    all_slices = exchange(
        0, state_send.at[others, message], state_recv.at[others, message], next_peer
    )
    all_scans = exchange(1, scan_send.at[others], scan_recv.at[others], next_peer)

    def each_peer(send):
        send(lax.rem(me + seq_size // 2, seq_size))

        def both_ways(d, carry):
            send(lax.rem(me + seq_size // 2 + d, seq_size))
            send(lax.rem(me + seq_size // 2 - d, seq_size))
            return carry

        lax.fori_loop(1, seq_size // 2, both_ways, 0)

    def send_slice(peer):
        exchange(0, state_send.at[peer, message], state_recv.at[me, message], peer).start()

    each_peer(send_slice)
    state_recv[me] = state_send[me]

    blocks = [lax.rem(row + 2, 4), lax.rem(row + 1, 4), lax.rem(row + 3, 4), row]
    order = [n // 2 + (n % 2) * SIDE for n in range(RING)]

    def columns(n):
        return slice(n * CHUNK, (n + 1) * CHUNK)

    loads[4].wait()

    def remote(src, dst, send_sem, recv_sem, device):
        return pltpu.make_async_remote_copy(
            src_ref=src, dst_ref=dst, send_sem=send_sem, recv_sem=recv_sem,
            device_id=device, device_id_type=MESH,
        )

    def paired_columns(part):
        return pl.ds(pl.multiple_of(RING * CHUNK + part * PAIRED, HEAD_DIM), PAIRED)

    deep = FEATURES // 2
    rows = pl.ds(pl.multiple_of(half * deep, deep), deep)
    quarter[...] = w[rows, paired_columns(x)].astype(F32)
    quarter_copies = [
        remote(quarter, w_mate.at[0, x, half], q_send.at[0], q_recv.at[0], (me, mate)),
        remote(
            w_mate.at[0, x, half], w_mate.at[0, x, half], q_send.at[1], q_recv.at[1],
            (z_pair, head),
        ),
    ]
    quarter_copies[0].start()
    parts = [x, lax.rem(x + 3, XS), lax.rem(x + 1, XS), lax.rem(x + 2, XS)]
    x_copies = []
    for i in range(2):
        x_copies.append([
            remote(
                w_mate.at[0, x, halves[i]], w_mate.at[0, x, halves[i]], x_send.at[side, i],
                x_recv.at[side, i],
                (peer, head),
            )
            for side, peer in ((0, x_up), (1, x_down))
        ])
    relay_up = remote(
        w_mate.at[0, parts[1], half], w_mate.at[0, parts[1], half], x_send.at[0, 2], x_recv.at[0, 2],
        (x_up, head),
    )
    relay_down = remote(
        w_mate.at[0, parts[2], 1 - half], w_mate.at[0, parts[2], 1 - half], x_send.at[1, 2], x_recv.at[1, 2],
        (x_down, head),
    )
    share_copies = [
        remote(w_mate.at[0, part], w_mate.at[1, part], d_send.at[j], d_recv.at[j], (me, partner))
        for j, part in enumerate(parts)
    ]

    pair_copies = {}
    for n in order:
        w_send[n] = w[:, columns(n)].astype(F32)
        pair_copies[n] = remote(
            w_send.at[n], w_recv.at[n], w_ssem.at[n], w_rsem.at[n], (me, partner)
        )
        pair_copies[n].start()
    for part in range(QUARTERS):
        p_send[part] = w[:, paired_columns(part)].astype(F32)
        pair_copies[RING + part] = remote(
            p_send.at[part], p_recv.at[part], w_ssem.at[RING + part], w_rsem.at[RING + part],
            (me, partner),
        )
        pair_copies[RING + part].start()

    def receive_weights(n):
        pair_copies[n].wait_recv()
        w_pair[:, columns(n)] = w_recv[n].astype(BF16)

    loads[3].wait()
    loads[5].wait()
    causal = low >= high

    def inside(b):
        rows = pl.ds(pl.multiple_of(b * BLOCK, BLOCK), BLOCK)
        for h in range(HEADS):
            scores = lax.dot_general(
                q[rows, head_columns(h)], k[rows, head_columns(h)], NT,
                preferred_element_type=F32,
            )
            run = run_col[b, :, h:h + 1]
            decay = jnp.exp(jnp.where(causal, run - run_row[b, h:h + 1, :], -1e30))
            weights = (scores * decay).astype(BF16)
            att[rows, head_columns(h)] = jnp.dot(
                weights, v[rows, head_columns(h)], preferred_element_type=F32
            )
            since[rows, head_columns(h)] = jnp.broadcast_to(jnp.exp(run), (BLOCK, HEAD_DIM))
            gate = g[rows, head_columns(h)].astype(F32)
            silu[rows, head_columns(h)] = gate / (1.0 + jnp.exp(-gate))

    inside(blocks[0])
    inside(blocks[1])

    all_slices.wait_recv()

    def scan(p, state):
        scan_send[p] = state
        return state_recv[p, slice_rows:slice_rows + 1, :] * state + state_recv[p, 0:slice_rows, :]

    lax.fori_loop(0, seq_size, scan, jnp.zeros((slice_rows, HEAD_DIM), F32), unroll=4)

    def send_scan(peer):
        exchange(1, scan_send.at[peer], scan_recv.at[me], peer).start()

    each_peer(send_scan)
    scan_recv[me] = scan_send[me]

    inside(blocks[2])
    inside(blocks[3])
    for n in order:
        receive_weights(n)
    quarter_copies[0].wait_recv()
    for copy in x_copies[0]:
        copy.start()
    all_scans.wait_recv()
    quarter_copies[1].start()

    hid_copies = []

    def hide(t):
        b = blocks[t]
        for h in range(HEADS):
            incoming = scan_recv[h * per_head:(h + 1) * per_head].reshape(HEAD_DIM, HEAD_DIM)
            state = start[b, h] + lead[b, h:h + 1, :] * incoming
            top = state.astype(BF16)
            entry[0, h] = top
            entry[1, h] = (state - top.astype(F32)).astype(BF16)
        for side in (1 - core, core):
            rows = pl.ds(pl.multiple_of(b * BLOCK + side * HALF, HALF), HALF)
            for h in range(HEADS):
                queries = q[rows, head_columns(h)]
                carried = jnp.dot(queries, entry[0, h], preferred_element_type=F32) + jnp.dot(
                    queries, entry[1, h], preferred_element_type=F32
                )
                attended = att[rows, head_columns(h)] + carried * since[rows, head_columns(h)]
                mean = jnp.mean(attended * attended, axis=-1, keepdims=True)
                gated = attended * lax.rsqrt(mean + 1e-6) * silu[rows, head_columns(h)]
                hid[t, side, :, head_columns(h)] = gated.astype(BF16).astype(F32)
            if side is not core:
                copy = pltpu.make_async_remote_copy(
                    src_ref=hid.at[t, 1 - core], dst_ref=hid_recv.at[t],
                    send_sem=h_ssem.at[t], recv_sem=h_rsem.at[t],
                    device_id=(me, partner), device_id_type=MESH,
                )
                copy.start()
                hid_copies.append(copy)

    def project(t, n):
        return jnp.dot(
            hid[t, core].astype(BF16), w[:, columns(n)], preferred_element_type=F32
        ) + jnp.dot(hid_recv[t].astype(BF16), w_pair[:, columns(n)], preferred_element_type=F32)

    def across(kind, n, src, dst, other):
        return pltpu.make_async_remote_copy(
            src_ref=src, dst_ref=dst, send_sem=y_send.at[kind, n], recv_sem=y_recv.at[kind, n],
            device_id=(me, other), device_id_type=MESH,
        )

    far_copies = [
        across(0, n, far.at[n], far_recv.at[n], up if n < SIDE else down) for n in range(RING)
    ]
    direct_copies = [
        across(
            1, n, minus.at[n] if n < SIDE else plus.at[n], direct_recv.at[n],
            down if n < SIDE else up,
        )
        for n in range(RING)
    ]
    sum_copies = [
        across(
            2, n, plus.at[n] if n < SIDE else minus.at[n], sum_recv.at[n],
            up if n < SIDE else down,
        )
        for n in range(RING)
    ]
    mate_turn, cross_turn = 1 + odd, 2 - odd
    mate_copies = []
    for block, t in enumerate((0, mate_turn)):
        for i, src in enumerate((hid.at[t, core], hid_recv.at[t])):
            mate_copies.append(
                remote(
                    src, hid_mate.at[block, i], m_send.at[block, i], m_recv.at[block, i], (me, mate)
                )
            )
    cross_copies = [
        remote(pair_out.at[j], pair_in.at[j], g_send.at[j], g_recv.at[j], (me, cross))
        for j in range(QUARTERS)
    ]

    def paired(block, t, part):
        products = (
            (hid[t, core], w[:, paired_columns(part)]),
            (hid_recv[t], p_recv[part].astype(BF16)),
            (hid_mate[block, 0], w_mate[0, part].reshape(FEATURES, PAIRED).astype(BF16)),
            (hid_mate[block, 1], w_mate[1, part].reshape(FEATURES, PAIRED).astype(BF16)),
        )
        total = jnp.zeros((HALF, PAIRED), F32)
        for left, right in products:
            total += jnp.dot(left.astype(BF16), right, preferred_element_type=F32)
        return total

    def cross_out(j):
        share_copies[j].wait_recv()
        pair_out[j] = paired(0, cross_turn, parts[j])
        cross_copies[j].start()

    hide(0)
    hid_copies[0].wait_recv()
    for n in order:
        far[n] = project(0, n)
        far_copies[n].start()
    for copy in mate_copies[:2]:
        copy.start()
    quarter_copies[1].wait_recv()
    for copy in x_copies[1]:
        copy.start()
    share_copies[0].start()
    hide(1)
    hide(2)
    hid_copies[1].wait_recv()
    for n in range(SIDE, RING):
        plus[n] = project(1, n)
        direct_copies[n].start()
    hid_copies[2].wait_recv()
    for n in range(SIDE):
        minus[n] = project(2, n)
        direct_copies[n].start()
    for copy in mate_copies[2:]:
        copy.start()
    x_copies[0][0].wait_recv()
    relay_up.start()
    for n in range(SIDE):
        plus[n] = project(1, n)
        minus[SIDE + n] = project(2, SIDE + n)
    hide(3)
    hid_copies[3].wait_recv()
    for n in order:
        own[n] = project(3, n)
    for n in range(SIDE):
        far_copies[n].wait_recv()
        plus[n] += far_recv[n]
        sum_copies[n].start()
        far_copies[SIDE + n].wait_recv()
        minus[SIDE + n] += far_recv[SIDE + n]
        sum_copies[SIDE + n].start()
    for part in range(QUARTERS):
        pair_copies[RING + part].wait_recv()
    for copy in mate_copies[:2]:
        copy.wait_recv()
    cross_out(0)
    x_copies[0][1].wait_recv()
    x_copies[1][1].wait_recv()
    relay_down.start()
    share_copies[2].start()
    x_copies[1][0].wait_recv()
    share_copies[1].start()
    cross_out(1)
    cross_out(2)
    relay_up.wait_recv()
    relay_down.wait_recv()
    share_copies[3].start()
    cross_out(3)
    for n in order:
        direct_copies[n].wait_recv()
        own[n] += direct_recv[n]
    for copy in mate_copies[2:]:
        copy.wait_recv()
    for j in range(QUARTERS):
        pair_own[j] = paired(1, 3, parts[j])

    for j, n in enumerate(order):
        cross_copies[j].wait_recv()
        out_ref[:, paired_columns(parts[j])] = (pair_own[j] + pair_in[j]).astype(BF16)
        sum_copies[n].wait_recv()
        out_ref[:, columns(n)] = (own[n] + sum_recv[n]).astype(BF16)

    all_slices.wait_send()
    all_scans.wait_send()
    for copy in list(pair_copies.values()) + hid_copies + far_copies + direct_copies + sum_copies:
        copy.wait_send()
    for copy in quarter_copies + x_copies[0] + x_copies[1] + [relay_up, relay_down]:
        copy.wait_send()
    for copy in share_copies + mate_copies + cross_copies:
        copy.wait_send()


def per_device(seq_size, queries, key_vectors, value_vectors, gate_input, log_decay, out_weight):
    tokens = BLOCKS * BLOCK
    slice_rows = FEATURES // seq_size
    whole = pl.BlockSpec(memory_space=pl.ANY)
    dma = pltpu.SemaphoreType.DMA
    vmem = pltpu.VMEM
    return pl.pallas_call(
        functools.partial(kernel, seq_size),
        out_shape=pltpu.VMEM((HALF, WIDTH), BF16),
        in_specs=[whole] * 6,
        out_specs=pl.BlockSpec(memory_space=pltpu.VMEM),
        scratch_shapes=[
            vmem((HEADS, tokens), F32),
            vmem((BLOCKS, 8, BLOCK), F32),
            vmem((tokens, FEATURES), BF16),
            vmem((tokens, FEATURES), BF16),
            vmem((tokens, FEATURES), BF16),
            vmem((tokens, FEATURES), BF16),
            vmem((FEATURES, WIDTH), BF16),
            vmem((RING, FEATURES, CHUNK), F32),
            vmem((RING, FEATURES, CHUNK), F32),
            vmem((QUARTERS, FEATURES, PAIRED), F32),
            vmem((QUARTERS, FEATURES, PAIRED), F32),
            vmem((FEATURES, RING * CHUNK), BF16),
            vmem((BLOCKS, BLOCK, 8), F32),
            vmem((BLOCKS, 8, BLOCK), F32),
            vmem((BLOCKS, HEADS, HEAD_DIM, HEAD_DIM), F32),
            vmem((BLOCKS, 8, HEAD_DIM), F32),
            vmem((seq_size, slice_rows + 8, HEAD_DIM), F32),
            vmem((seq_size, slice_rows + 8, HEAD_DIM), F32),
            vmem((seq_size, slice_rows, HEAD_DIM), F32),
            vmem((seq_size, slice_rows, HEAD_DIM), F32),
            vmem((tokens, FEATURES), F32),
            vmem((tokens, FEATURES), F32),
            vmem((tokens, FEATURES), F32),
            vmem((2, HEADS, HEAD_DIM, HEAD_DIM), BF16),
            vmem((BLOCKS, 2, HALF, FEATURES), F32),
            vmem((BLOCKS, HALF, FEATURES), F32),
            vmem((RING, HALF, CHUNK), F32),
            vmem((RING, HALF, CHUNK), F32),
            vmem((RING, HALF, CHUNK), F32),
            vmem((RING, HALF, CHUNK), F32),
            vmem((RING, HALF, CHUNK), F32),
            vmem((RING, HALF, CHUNK), F32),
            vmem((RING, HALF, CHUNK), F32),
            vmem((FEATURES // 2, PAIRED), F32),
            vmem((2, QUARTERS, 2, FEATURES // 2, PAIRED), F32),
            vmem((2, 2, HALF, FEATURES), F32),
            vmem((QUARTERS, HALF, PAIRED), F32),
            vmem((QUARTERS, HALF, PAIRED), F32),
            vmem((QUARTERS, HALF, PAIRED), F32),
            dma((6,)), dma((2,)), dma((2,)), dma((RING + QUARTERS,)), dma((RING + QUARTERS,)), dma((BLOCKS,)), dma((BLOCKS,)),
            dma((3, RING)), dma((3, RING)),
            pltpu.SemaphoreType.REGULAR, dma((2,)), dma((2,)), dma((2, 3)), dma((2, 3)),
            dma((QUARTERS,)), dma((QUARTERS,)), dma((2, 2)), dma((2, 2)),
            dma((QUARTERS,)), dma((QUARTERS,)),
        ],
        compiler_params=pltpu.CompilerParams(
            collective_id=0, has_side_effects=True, vmem_limit_bytes=62 * 1024 * 1024
        ),
    )(log_decay.T, key_vectors, value_vectors, queries, gate_input, out_weight)


def solution(mesh):
    placed = (
        P("seq", "head"),
        P("seq", "head"),
        P("seq", "head"),
        P("seq", "head"),
        P("seq", "head"),
        P("head", None),
    )
    return jax.shard_map(
        functools.partial(per_device, mesh.shape["seq"]),
        mesh=mesh, in_specs=placed, out_specs=P(("seq", "head"), None), check_vma=False,
    )
```

```python
import functools

import jax
import jax.numpy as jnp
from jax import lax
from jax.experimental import pallas as pl
from jax.experimental.pallas import tpu as pltpu
from jax.sharding import PartitionSpec as P

HEAD_DIM = 128
BLOCK = 256
HALF = 128
HEADS = 4
BLOCKS = 4
FEATURES = HEADS * HEAD_DIM
WIDTH = 4096
CHUNK = 512
CHUNKS = WIDTH // CHUNK
RING = CHUNKS // 2
SIDE = RING // 2
QUARTERS = CHUNKS - RING
XS = 4
F32 = jnp.float32
BF16 = jnp.bfloat16
MESH = pl.DeviceIdType.MESH
NT = (((1,), (1,)), ((), ()))
TN = (((0,), (0,)), ((), ()))


def head_columns(h):
    return slice(h * HEAD_DIM, (h + 1) * HEAD_DIM)


def kernel(
    seq_size, rate_hbm, k_hbm, v_hbm, q_hbm, g_hbm, w_hbm, out_ref,
    rate, padded, k, v, q, g, w, w_send, w_recv, w_pair,
    run_col, run_row, start, lead, state_send, state_recv, scan_send, scan_recv,
    att, since, silu, entry, hid, hid_recv, far, plus, minus, own, far_recv, direct_recv,
    sum_recv, quarter, w_mate, hid_mate, pair_out, pair_in, pair_own,
    load_sem, a_send, a_recv, w_ssem, w_rsem, h_ssem, h_rsem,
    y_send, y_recv, line_sem, q_send, q_recv, x_send, x_recv, d_send, d_recv,
    m_send, m_recv, g_send, g_recv,
):
    me = lax.axis_index("seq")
    head = lax.axis_index("head")
    row = head // 2
    core = lax.rem(head, 2)
    partner = row * 2 + (1 - core)
    up = lax.rem(row + 1, 4) * 2 + core
    down = lax.rem(row + 3, 4) * 2 + core
    slice_rows = FEATURES // seq_size
    per_head = HEAD_DIM // slice_rows
    odd = lax.rem(row, 2)
    mate = (row + 1 - 2 * odd) * 2 + core
    cross = lax.rem(row + 3 + 2 * odd, 4) * 2 + core
    x = lax.rem(me, XS)
    x_up = me - x + lax.rem(x + 1, XS)
    x_down = me - x + lax.rem(x + 3, XS)
    half = lax.rem(me // XS, 2)
    z_pair = me + XS * (1 - 2 * half)
    halves = (half, 1 - half)

    loads = [
        pltpu.make_async_copy(src, dst, load_sem.at[i])
        for i, (src, dst) in enumerate(
            ((rate_hbm, rate), (k_hbm, k), (v_hbm, v), (q_hbm, q), (w_hbm, w), (g_hbm, g))
        )
    ]
    for load in loads[:3]:
        load.start()

    barrier = pltpu.get_barrier_semaphore()

    def greet(peer):
        pl.semaphore_signal(barrier, inc=1, device_id=(peer, head), device_id_type=MESH)

    zs = seq_size // XS
    x_line = [me - x + lax.rem(x + d, XS) for d in range(1, XS)]
    for peer in x_line:
        greet(peer)
    for d in range(1, zs):
        greet(lax.rem(me + d * XS, seq_size))
    for other in (partner, up, down):
        pl.semaphore_signal(barrier, inc=1, device_id=(me, other), device_id_type=MESH)

    low = lax.broadcasted_iota(jnp.int32, (BLOCK, BLOCK), 0)
    high = lax.broadcasted_iota(jnp.int32, (BLOCK, BLOCK), 1)
    upper = jnp.where(low <= high, 1.0, 0.0).astype(BF16)
    lower = jnp.where(low >= high, 1.0, 0.0).astype(BF16)
    loads[0].wait()
    for b in range(BLOCKS):
        padded[b, 0:HEADS, :] = rate[:, b * BLOCK:(b + 1) * BLOCK]
        padded[b, HEADS:8, :] = jnp.zeros((8 - HEADS, BLOCK), F32)
    rates = padded[...].reshape(BLOCKS * 8, BLOCK)
    run_rows = jnp.zeros((BLOCKS * 8, BLOCK), F32)
    run_cols = jnp.zeros((BLOCK, BLOCKS * 8), F32)
    for _ in range(3):
        piece = rates.astype(BF16)
        run_rows += jnp.dot(piece, upper, preferred_element_type=F32)
        run_cols += lax.dot_general(lower, piece, NT, preferred_element_type=F32)
        rates = rates - piece.astype(F32)
    run_row[...] = run_rows.reshape(BLOCKS, 8, BLOCK)
    for b in range(BLOCKS):
        run_col[b] = run_cols[:, 8 * b:8 * b + 8]
    totals = run_rows[:, BLOCK - 1:BLOCK]
    key_scale = jnp.exp(totals - run_rows)
    block_decay = jnp.broadcast_to(jnp.exp(totals), (BLOCKS * 8, HEAD_DIM))
    ahead = jnp.zeros((8, 1), F32)
    for b in range(BLOCKS):
        lead[b] = jnp.broadcast_to(jnp.exp(ahead), (8, HEAD_DIM))
        ahead = ahead + totals[8 * b:8 * b + 8]
    through = jnp.broadcast_to(jnp.exp(ahead), (8, HEAD_DIM))
    pl.semaphore_wait(barrier, XS - 1 + zs - 1 + 3)
    for peer in x_line:
        pl.semaphore_signal(line_sem, inc=1, device_id=(peer, head), device_id_type=MESH)
    loads[1].wait()
    loads[2].wait()
    for load in loads[3:]:
        load.start()
    for h in range(HEADS):
        state = jnp.zeros((HEAD_DIM, HEAD_DIM), F32)
        for b in range(BLOCKS):
            rows = slice(b * BLOCK, (b + 1) * BLOCK)
            line = slice(8 * b + h, 8 * b + h + 1)
            start[b, h] = state
            keys = (k[rows, head_columns(h)].T.astype(F32) * key_scale[line]).astype(BF16)
            added = jnp.dot(keys, v[rows, head_columns(h)], preferred_element_type=F32)
            state = block_decay[line] * state + added
        pieces = pl.ds(h * per_head, per_head)
        state_send[pieces, 0:slice_rows, :] = state.reshape(per_head, slice_rows, HEAD_DIM)
        state_send[pieces, slice_rows:slice_rows + 8, :] = jnp.broadcast_to(
            through[h:h + 1], (per_head, 8, HEAD_DIM)
        )

    pl.semaphore_wait(line_sem, XS - 1)

    def exchange(phase, src, dst, peer):
        return pltpu.make_async_remote_copy(
            src_ref=src, dst_ref=dst, send_sem=a_send.at[phase], recv_sem=a_recv.at[phase],
            device_id=(peer, head), device_id_type=MESH,
        )

    others = pl.ds(0, seq_size - 1)
    next_peer = lax.rem(me + 1, seq_size)
    message = pl.ds(0, slice_rows + 1)
    all_slices = exchange(
        0, state_send.at[others, message], state_recv.at[others, message], next_peer
    )
    all_scans = exchange(1, scan_send.at[others], scan_recv.at[others], next_peer)

    def each_peer(send):
        send(lax.rem(me + seq_size // 2, seq_size))

        def both_ways(d, carry):
            send(lax.rem(me + seq_size // 2 + d, seq_size))
            send(lax.rem(me + seq_size // 2 - d, seq_size))
            return carry

        lax.fori_loop(1, seq_size // 2, both_ways, 0)

    def send_slice(peer):
        exchange(0, state_send.at[peer, message], state_recv.at[me, message], peer).start()

    each_peer(send_slice)
    state_recv[me] = state_send[me]

    blocks = [lax.rem(row + 2, 4), lax.rem(row + 1, 4), lax.rem(row + 3, 4), row]
    order = [n // 2 + (n % 2) * SIDE for n in range(RING)]

    def columns(n):
        return slice(n * CHUNK, (n + 1) * CHUNK)

    loads[4].wait()

    def remote(src, dst, send_sem, recv_sem, device):
        return pltpu.make_async_remote_copy(
            src_ref=src, dst_ref=dst, send_sem=send_sem, recv_sem=recv_sem,
            device_id=device, device_id_type=MESH,
        )

    def paired_columns(part):
        return pl.ds(pl.multiple_of((RING + part) * CHUNK, CHUNK), CHUNK)

    deep = FEATURES // 2
    rows = pl.ds(pl.multiple_of(half * deep, deep), deep)
    quarter[...] = w[rows, paired_columns(x)].astype(F32)
    quarter_copies = [
        remote(quarter, w_mate.at[0, x, half], q_send.at[0], q_recv.at[0], (me, mate)),
        remote(
            w_mate.at[0, x, half], w_mate.at[0, x, half], q_send.at[1], q_recv.at[1],
            (z_pair, head),
        ),
    ]
    quarter_copies[0].start()
    parts = [x, lax.rem(x + 3, XS), lax.rem(x + 1, XS), lax.rem(x + 2, XS)]
    x_copies = []
    for i in range(2):
        x_copies.append([
            remote(
                w_mate.at[0, x, halves[i]], w_mate.at[0, x, halves[i]], x_send.at[side, i],
                x_recv.at[side, i],
                (peer, head),
            )
            for side, peer in ((0, x_up), (1, x_down))
        ])
    relay_up = remote(
        w_mate.at[0, parts[1], half], w_mate.at[0, parts[1], half], x_send.at[0, 2], x_recv.at[0, 2],
        (x_up, head),
    )
    relay_down = remote(
        w_mate.at[0, parts[2], 1 - half], w_mate.at[0, parts[2], 1 - half], x_send.at[1, 2], x_recv.at[1, 2],
        (x_down, head),
    )
    share_copies = [
        remote(w_mate.at[0, part], w_mate.at[1, part], d_send.at[j], d_recv.at[j], (me, partner))
        for j, part in enumerate(parts)
    ]

    pair_copies = {}
    for n in order + list(range(RING, CHUNKS)):
        w_send[n] = w[:, columns(n)].astype(F32)
        pair_copies[n] = pltpu.make_async_remote_copy(
            src_ref=w_send.at[n], dst_ref=w_recv.at[n],
            send_sem=w_ssem.at[n], recv_sem=w_rsem.at[n],
            device_id=(me, partner), device_id_type=MESH,
        )
        pair_copies[n].start()

    def receive_weights(n):
        pair_copies[n].wait_recv()
        w_pair[:, columns(n)] = w_recv[n].astype(BF16)

    loads[3].wait()
    loads[5].wait()
    causal = low >= high

    def inside(b):
        rows = pl.ds(pl.multiple_of(b * BLOCK, BLOCK), BLOCK)
        for h in range(HEADS):
            scores = lax.dot_general(
                q[rows, head_columns(h)], k[rows, head_columns(h)], NT,
                preferred_element_type=F32,
            )
            run = run_col[b, :, h:h + 1]
            decay = jnp.exp(jnp.where(causal, run - run_row[b, h:h + 1, :], -1e30))
            weights = (scores * decay).astype(BF16)
            att[rows, head_columns(h)] = jnp.dot(
                weights, v[rows, head_columns(h)], preferred_element_type=F32
            )
            since[rows, head_columns(h)] = jnp.broadcast_to(jnp.exp(run), (BLOCK, HEAD_DIM))
            gate = g[rows, head_columns(h)].astype(F32)
            silu[rows, head_columns(h)] = gate / (1.0 + jnp.exp(-gate))

    inside(blocks[0])
    inside(blocks[1])

    all_slices.wait_recv()

    def scan(p, state):
        scan_send[p] = state
        return state_recv[p, slice_rows:slice_rows + 1, :] * state + state_recv[p, 0:slice_rows, :]

    lax.fori_loop(0, seq_size, scan, jnp.zeros((slice_rows, HEAD_DIM), F32), unroll=4)

    def send_scan(peer):
        exchange(1, scan_send.at[peer], scan_recv.at[me], peer).start()

    each_peer(send_scan)
    scan_recv[me] = scan_send[me]

    inside(blocks[2])
    inside(blocks[3])
    for n in order:
        receive_weights(n)
    quarter_copies[0].wait_recv()
    for copy in x_copies[0]:
        copy.start()
    all_scans.wait_recv()
    quarter_copies[1].start()

    hid_copies = []

    def hide(t):
        b = blocks[t]
        for h in range(HEADS):
            incoming = scan_recv[h * per_head:(h + 1) * per_head].reshape(HEAD_DIM, HEAD_DIM)
            state = start[b, h] + lead[b, h:h + 1, :] * incoming
            top = state.astype(BF16)
            entry[0, h] = top
            entry[1, h] = (state - top.astype(F32)).astype(BF16)
        for side in (1 - core, core):
            rows = pl.ds(pl.multiple_of(b * BLOCK + side * HALF, HALF), HALF)
            for h in range(HEADS):
                queries = q[rows, head_columns(h)]
                carried = jnp.dot(queries, entry[0, h], preferred_element_type=F32) + jnp.dot(
                    queries, entry[1, h], preferred_element_type=F32
                )
                attended = att[rows, head_columns(h)] + carried * since[rows, head_columns(h)]
                mean = jnp.mean(attended * attended, axis=-1, keepdims=True)
                gated = attended * lax.rsqrt(mean + 1e-6) * silu[rows, head_columns(h)]
                hid[t, side, :, head_columns(h)] = gated.astype(BF16).astype(F32)
            if side is not core:
                copy = pltpu.make_async_remote_copy(
                    src_ref=hid.at[t, 1 - core], dst_ref=hid_recv.at[t],
                    send_sem=h_ssem.at[t], recv_sem=h_rsem.at[t],
                    device_id=(me, partner), device_id_type=MESH,
                )
                copy.start()
                hid_copies.append(copy)

    def project(t, n):
        return jnp.dot(
            hid[t, core].astype(BF16), w[:, columns(n)], preferred_element_type=F32
        ) + jnp.dot(hid_recv[t].astype(BF16), w_pair[:, columns(n)], preferred_element_type=F32)

    def across(kind, n, src, dst, other):
        return pltpu.make_async_remote_copy(
            src_ref=src, dst_ref=dst, send_sem=y_send.at[kind, n], recv_sem=y_recv.at[kind, n],
            device_id=(me, other), device_id_type=MESH,
        )

    far_copies = [
        across(0, n, far.at[n], far_recv.at[n], up if n < SIDE else down) for n in range(RING)
    ]
    direct_copies = [
        across(
            1, n, minus.at[n] if n < SIDE else plus.at[n], direct_recv.at[n],
            down if n < SIDE else up,
        )
        for n in range(RING)
    ]
    sum_copies = [
        across(
            2, n, plus.at[n] if n < SIDE else minus.at[n], sum_recv.at[n],
            up if n < SIDE else down,
        )
        for n in range(RING)
    ]
    mate_turn, cross_turn = 1 + odd, 2 - odd
    mate_copies = []
    for block, t in enumerate((0, mate_turn)):
        for i, src in enumerate((hid.at[t, core], hid_recv.at[t])):
            mate_copies.append(
                remote(
                    src, hid_mate.at[block, i], m_send.at[block, i], m_recv.at[block, i], (me, mate)
                )
            )
    cross_copies = [
        remote(pair_out.at[j], pair_in.at[j], g_send.at[j], g_recv.at[j], (me, cross))
        for j in range(QUARTERS)
    ]

    def paired(block, t, part):
        products = (
            (hid[t, core], w[:, paired_columns(part)]),
            (hid_recv[t], w_recv[RING + part].astype(BF16)),
            (hid_mate[block, 0], w_mate[0, part].reshape(FEATURES, CHUNK).astype(BF16)),
            (hid_mate[block, 1], w_mate[1, part].reshape(FEATURES, CHUNK).astype(BF16)),
        )
        total = jnp.zeros((HALF, CHUNK), F32)
        for left, right in products:
            total += jnp.dot(left.astype(BF16), right, preferred_element_type=F32)
        return total

    def cross_out(j):
        share_copies[j].wait_recv()
        pair_out[j] = paired(0, cross_turn, parts[j])
        cross_copies[j].start()

    hide(0)
    mate_copies[0].start()
    hid_copies[0].wait_recv()
    for n in order:
        far[n] = project(0, n)
        far_copies[n].start()
    mate_copies[1].start()
    quarter_copies[1].wait_recv()
    for copy in x_copies[1]:
        copy.start()
    share_copies[0].start()
    hide(1)
    hide(2)
    hid_copies[1].wait_recv()
    for n in range(SIDE, RING):
        plus[n] = project(1, n)
        direct_copies[n].start()
    hid_copies[2].wait_recv()
    for n in range(SIDE):
        minus[n] = project(2, n)
        direct_copies[n].start()
    for copy in mate_copies[2:]:
        copy.start()
    x_copies[0][0].wait_recv()
    relay_up.start()
    for n in range(SIDE):
        plus[n] = project(1, n)
        minus[SIDE + n] = project(2, SIDE + n)
    hide(3)
    hid_copies[3].wait_recv()
    for n in order:
        own[n] = project(3, n)
    for n in range(SIDE):
        far_copies[n].wait_recv()
        plus[n] += far_recv[n]
        sum_copies[n].start()
        far_copies[SIDE + n].wait_recv()
        minus[SIDE + n] += far_recv[SIDE + n]
        sum_copies[SIDE + n].start()
    for n in range(RING, CHUNKS):
        pair_copies[n].wait_recv()
    x_copies[0][1].wait_recv()
    x_copies[1][1].wait_recv()
    relay_down.start()
    share_copies[2].start()
    x_copies[1][0].wait_recv()
    share_copies[1].start()
    for copy in mate_copies[:2]:
        copy.wait_recv()
    cross_out(0)
    cross_out(1)
    cross_out(2)
    relay_up.wait_recv()
    relay_down.wait_recv()
    share_copies[3].start()
    cross_out(3)
    for n in order:
        direct_copies[n].wait_recv()
        own[n] += direct_recv[n]
    for copy in mate_copies[2:]:
        copy.wait_recv()
    for j in range(QUARTERS):
        pair_own[j] = paired(1, 3, parts[j])

    for j, n in enumerate(order):
        cross_copies[j].wait_recv()
        out_ref[:, paired_columns(parts[j])] = (pair_own[j] + pair_in[j]).astype(BF16)
        sum_copies[n].wait_recv()
        out_ref[:, columns(n)] = (own[n] + sum_recv[n]).astype(BF16)

    all_slices.wait_send()
    all_scans.wait_send()
    for copy in list(pair_copies.values()) + hid_copies + far_copies + direct_copies + sum_copies:
        copy.wait_send()
    for copy in quarter_copies + x_copies[0] + x_copies[1] + [relay_up, relay_down]:
        copy.wait_send()
    for copy in share_copies + mate_copies + cross_copies:
        copy.wait_send()


def per_device(seq_size, queries, key_vectors, value_vectors, gate_input, log_decay, out_weight):
    tokens = BLOCKS * BLOCK
    slice_rows = FEATURES // seq_size
    whole = pl.BlockSpec(memory_space=pl.ANY)
    dma = pltpu.SemaphoreType.DMA
    vmem = pltpu.VMEM
    return pl.pallas_call(
        functools.partial(kernel, seq_size),
        out_shape=pltpu.VMEM((HALF, WIDTH), BF16),
        in_specs=[whole] * 6,
        out_specs=pl.BlockSpec(memory_space=pltpu.VMEM),
        scratch_shapes=[
            vmem((HEADS, tokens), F32),
            vmem((BLOCKS, 8, BLOCK), F32),
            vmem((tokens, FEATURES), BF16),
            vmem((tokens, FEATURES), BF16),
            vmem((tokens, FEATURES), BF16),
            vmem((tokens, FEATURES), BF16),
            vmem((FEATURES, WIDTH), BF16),
            vmem((CHUNKS, FEATURES, CHUNK), F32),
            vmem((CHUNKS, FEATURES, CHUNK), F32),
            vmem((FEATURES, RING * CHUNK), BF16),
            vmem((BLOCKS, BLOCK, 8), F32),
            vmem((BLOCKS, 8, BLOCK), F32),
            vmem((BLOCKS, HEADS, HEAD_DIM, HEAD_DIM), F32),
            vmem((BLOCKS, 8, HEAD_DIM), F32),
            vmem((seq_size, slice_rows + 8, HEAD_DIM), F32),
            vmem((seq_size, slice_rows + 8, HEAD_DIM), F32),
            vmem((seq_size, slice_rows, HEAD_DIM), F32),
            vmem((seq_size, slice_rows, HEAD_DIM), F32),
            vmem((tokens, FEATURES), F32),
            vmem((tokens, FEATURES), F32),
            vmem((tokens, FEATURES), F32),
            vmem((2, HEADS, HEAD_DIM, HEAD_DIM), BF16),
            vmem((BLOCKS, 2, HALF, FEATURES), F32),
            vmem((BLOCKS, HALF, FEATURES), F32),
            vmem((RING, HALF, CHUNK), F32),
            vmem((RING, HALF, CHUNK), F32),
            vmem((RING, HALF, CHUNK), F32),
            vmem((RING, HALF, CHUNK), F32),
            vmem((RING, HALF, CHUNK), F32),
            vmem((RING, HALF, CHUNK), F32),
            vmem((RING, HALF, CHUNK), F32),
            vmem((FEATURES // 2, CHUNK), F32),
            vmem((2, QUARTERS, 2, FEATURES // 2, CHUNK), F32),
            vmem((2, 2, HALF, FEATURES), F32),
            vmem((QUARTERS, HALF, CHUNK), F32),
            vmem((QUARTERS, HALF, CHUNK), F32),
            vmem((QUARTERS, HALF, CHUNK), F32),
            dma((6,)), dma((2,)), dma((2,)), dma((CHUNKS,)), dma((CHUNKS,)), dma((BLOCKS,)), dma((BLOCKS,)),
            dma((3, RING)), dma((3, RING)),
            pltpu.SemaphoreType.REGULAR, dma((2,)), dma((2,)), dma((2, 3)), dma((2, 3)),
            dma((QUARTERS,)), dma((QUARTERS,)), dma((2, 2)), dma((2, 2)),
            dma((QUARTERS,)), dma((QUARTERS,)),
        ],
        compiler_params=pltpu.CompilerParams(
            collective_id=0, has_side_effects=True, vmem_limit_bytes=62 * 1024 * 1024
        ),
    )(log_decay.T, key_vectors, value_vectors, queries, gate_input, out_weight)


def solution(mesh):
    placed = (
        P("seq", "head"),
        P("seq", "head"),
        P("seq", "head"),
        P("seq", "head"),
        P("seq", "head"),
        P("head", None),
    )
    return jax.shard_map(
        functools.partial(per_device, mesh.shape["seq"]),
        mesh=mesh, in_specs=placed, out_specs=P(("seq", "head"), None), check_vma=False,
    )
```
